256 devices in a mesh: wide: 16 (over z_lo, x, core), long: 16 (over y, z_hi).
Axes of the slice: x: 4, y: 4, z: 8 (z_hi: 4, z_lo: 2; z = z_hi * 2 + z_lo), core: 2. Of those that a mesh axis runs over, the one named last changes fastest.
Arguments:
- slab_vertices: float32 [3, 4096], P(None, 'wide'), may hold values from 0 to 1
- slab_elements: int32 [3, 8192], P(None, 'wide'), may hold values from 0 to 4095, as said below
- source_vertices: float32 [3, 16384], P(None, ('wide', 'long')), may hold values from 0 to 1
- source_elements: int32 [3, 32768], P(None, ('wide', 'long')), may hold values from 0 to 16383, as said below
- primal_basis: bfloat16 [32, 32768], P(None, ('wide', 'long')), may hold values from -12 to 12
- adjoint_basis: bfloat16 [32, 8192], P(None, 'wide'), may hold values from -24 to 24
Outputs:
- primal_image: float32 [32, 8192], P(None, ('wide', 'long'))
- adjoint_image: float32 [32, 32768], P(None, ('wide', 'long'))
The draws below stay inside these ranges and needn't reach their ends.
Inputs may be any that keep to these rules, and one draw needn't show every extreme that they name: `slab_elements`: a slab triangle in columns b * 512 to (b + 1) * 512 - 1 names only vertices b * 256 to (b + 1) * 256 - 1; both ends of each such range are named. `source_elements`: a source triangle in columns b * 128 to (b + 1) * 128 - 1 names only vertices b * 64 to (b + 1) * 64 - 1; both ends of each such range are named.
All inputs are finite; a program needn't handle non-finite values.
Results may differ from the reference program's by a relative error of at most 0.0029.
Values may be sent and summed in bfloat16 or wider, within the bound.
A program may use at most 64 MiB of HBM per device.

```python
import math
import jax
import jax.numpy as jnp
from jax import lax

BASIS = 16
SLAB_W = 512
SRC_DEV = 128
SLAB = 8192
SOURCES = 32768


def block_connectivity(key, total, block):
    half_block = block // 2
    columns = jnp.arange(total, dtype=jnp.int32)[None, :]
    corner_row = jnp.arange(3, dtype=jnp.int32)[:, None]
    base_ids = columns // block * half_block
    offsets = jax.random.randint(jax.random.fold_in(key, 17), (3, total), 0, half_block, dtype=jnp.int32)
    values = base_ids + offsets
    values = jnp.where((corner_row == 0) & (columns % block == 0), base_ids, values)
    values = jnp.where((corner_row == 2) & (columns % block == block - 1), base_ids + half_block - 1, values)
    return values


def draw_slab_elements(key, part):
    return block_connectivity(key, SLAB, SLAB_W)


def draw_source_elements(key, part):
    return block_connectivity(key, SOURCES, SRC_DEV)


def block_scale(rng, dims, split, least, largest):
    loudness, own = 1.0, jax.random.fold_in(rng, 6)
    for position, blocks in split:
        heights = jnp.exp(jax.random.uniform(jax.random.fold_in(own, position), (blocks,), jnp.float32, least / len(split), largest / len(split)))
        loudness = loudness * jnp.repeat(heights, dims[position] // blocks).reshape([-1 if axis == position else 1 for axis in range(len(dims))])
    return loudness


def normal_values(own_key, shape, scale, limit, cuts=(), kind=jnp.bfloat16):
    values = scale * jax.random.normal(own_key, shape, jnp.float32)
    if cuts:
        values = values * block_scale(own_key, shape, cuts, -0.22, 0.18)
    return jnp.clip(values, -limit, limit).astype(kind)


def setup_inputs(seed: int = 0) -> dict:
    key_list = jax.random.split(jax.random.key(seed), 7)
    return {
        "slab_vertices": jnp.clip(1.0 * jax.random.uniform(key_list[0], (3, SLAB // 2), jnp.float32) ** block_scale(key_list[0], (3, SLAB // 2), ((1, 16),), -0.2, 0.2), 0.0, 1.0),
        "slab_elements": draw_slab_elements(jax.random.fold_in(key_list[6], 71), 0),
        "source_vertices": jnp.clip(1.0 * jax.random.uniform(key_list[2], (3, SOURCES // 2), jnp.float32) ** block_scale(key_list[2], (3, SOURCES // 2), ((1, 256),), -0.2, 0.2), 0.0, 1.0),
        "source_elements": draw_source_elements(jax.random.fold_in(key_list[6], 71), 0),
        "primal_basis": normal_values(key_list[4], (2 * BASIS, SOURCES), 2.0, 12.0, ((1, 256),)),
        "adjoint_basis": normal_values(key_list[5], (2 * BASIS, SLAB), 4.0, 24.0, ((1, 16),)),
    }


WAVENUMBER = 40.0
SOFTENING = 0.0004
AREA_WEIGHT = 0.05
FOUR_PI = 4.0 * math.pi

def geometry(vertices, elements):
    corners = [jnp.take(vertices, elements[corner], axis=1) for corner in range(3)]
    centre = (corners[0] + corners[1] + corners[2]) / 3.0
    edge_one = corners[1] - corners[0]
    edge_two = corners[2] - corners[0]
    normal_x = edge_one[1] * edge_two[2] - edge_one[2] * edge_two[1]
    normal_y = edge_one[2] * edge_two[0] - edge_one[0] * edge_two[2]
    normal_z = edge_one[0] * edge_two[1] - edge_one[1] * edge_two[0]
    areas = 0.5 * jnp.sqrt(normal_x * normal_x + normal_y * normal_y + normal_z * normal_z)
    return jnp.concatenate([centre, areas[None, :]], axis=0)

def kernel_tile(targets, sources):
    spread = targets[0][:, None] - sources[0][None, :]
    square_sum = spread * spread
    for axis_id in range(1, 3):
        spread = targets[axis_id][:, None] - sources[axis_id][None, :]
        square_sum = square_sum + spread * spread
    radius = jnp.sqrt(square_sum + SOFTENING + AREA_WEIGHT * (targets[3][:, None] + sources[3][None, :]))
    weight = targets[3][:, None] * sources[3][None, :] / (FOUR_PI * radius)
    phases = WAVENUMBER * radius
    return ((weight * jnp.cos(phases)).astype(jnp.bfloat16), (weight * jnp.sin(phases)).astype(jnp.bfloat16))

def pack_primal(columns):
    half_rows = columns.shape[0] // 2
    real_part = columns[:half_rows]
    imag_part = columns[half_rows:]
    return jnp.concatenate([jnp.concatenate([real_part, -imag_part], 1), jnp.concatenate([imag_part, real_part], 1)], 0)

def pack_adjoint(row_block):
    half_rows = row_block.shape[0] // 2
    real_part = row_block[:half_rows]
    imag_part = row_block[half_rows:]
    return jnp.concatenate([jnp.concatenate([real_part, imag_part], 1), jnp.concatenate([imag_part, -real_part], 1)], 0)

def primal_part(primal_pack, tile_real, tile_imag):
    stacked = jnp.concatenate([tile_real, tile_imag], 1)
    return jnp.dot(primal_pack, stacked.T, preferred_element_type=jnp.float32)

def adjoint_part(adjoint_pack, tile_real, tile_imag):
    stacked = jnp.concatenate([tile_real, tile_imag], 0)
    return jnp.dot(adjoint_pack, stacked, preferred_element_type=jnp.float32)

def reference(slab_vertices, slab_elements, source_vertices, source_elements, primal_basis, adjoint_basis):
    slab_points = geometry(slab_vertices, slab_elements)
    source_points = geometry(source_vertices, source_elements)
    block_count = SOURCES // SRC_DEV
    source_blocks = source_points.reshape(4, block_count, SRC_DEV).transpose(1, 0, 2)
    basis_blocks = primal_basis.reshape(2 * BASIS, block_count, SRC_DEV).transpose(1, 0, 2)
    adjoint_pack = pack_adjoint(adjoint_basis)

    def advance(running, blocked):
        points, columns = blocked
        tile_real, tile_imag = kernel_tile(slab_points, points)
        running = running + primal_part(pack_primal(columns), tile_real, tile_imag)
        return (running, adjoint_part(adjoint_pack, tile_real, tile_imag))
    summed, adjoint_blocks = lax.scan(advance, jnp.zeros((2 * BASIS, SLAB), jnp.float32), (source_blocks, basis_blocks))
    adjoint_image = adjoint_blocks.transpose(1, 0, 2).reshape(2 * BASIS, SOURCES)
    return (summed, adjoint_image)
```

```python
import functools
import math

import jax
import jax.numpy as jnp
from jax import lax
from jax.experimental import pallas as pl
from jax.experimental.pallas import tpu as pltpu
from jax.sharding import PartitionSpec as P

WAVENUMBER = 40.0
SOFTENING = 0.0004
AREA_WEIGHT = 0.05
TURNS = WAVENUMBER / (2.0 * math.pi)
SCALE = TURNS * TURNS
WEIGHT = TURNS / (4.0 * math.pi)
ROUND = 12582912.0
ROOT2 = math.sqrt(2.0)
SIN = tuple(ROOT2 * c for c in (3.14158202, -5.16714279, 2.54189895, -0.55463599))
COS = tuple(ROOT2 * c for c in (0.99999995, -4.93479286, 4.05841191, -1.33188013, 0.21969673))
ROWS = 48
MESH = pl.DeviceIdType.MESH
F32 = jnp.float32
BF16 = jnp.bfloat16


def split3(x):
    one = x.astype(BF16).astype(F32)
    rest = x - one
    two = rest.astype(BF16).astype(F32)
    three = (rest - two).astype(BF16).astype(F32)
    return one, two, three


def points(padded, ids, anchor):
    count, width = padded.shape[1], ids.shape[1]
    parts = jnp.concatenate(split3(padded), axis=0).astype(BF16)
    rows = lax.broadcasted_iota(jnp.int32, (count, width), 0) + anchor
    corners = []
    for corner in range(3):
        chosen = jnp.where(rows == ids[corner : corner + 1, :], 1.0, 0.0).astype(BF16)
        found = jnp.dot(parts, chosen, preferred_element_type=F32)
        corners.append(found[0:8] + found[8:16] + found[16:24])
    centre = (corners[0] + corners[1] + corners[2]) * (1.0 / 3.0) - 0.5
    one = corners[1] - corners[0]
    two = corners[2] - corners[0]
    ox, oy, oz = one[0:1], one[1:2], one[2:3]
    tx, ty, tz = two[0:1], two[1:2], two[2:3]
    nx = oy * tz - oz * ty
    ny = oz * tx - ox * tz
    nz = ox * ty - oy * tx
    area = 0.5 * jnp.sqrt(nx * nx + ny * ny + nz * nz)
    square = centre * centre
    norm = square[0:1] + square[1:2] + square[2:3]
    return centre, area, norm


def tile_values(scaled, weight):
    inverse = lax.rsqrt(scaled)
    turns = scaled * inverse
    part = turns - ((turns + ROUND) - ROUND)
    square = part * part
    sine = SIN[3]
    for c in SIN[2::-1]:
        sine = sine * square + c
    sine = sine * part
    cosine = COS[4]
    for c in COS[3::-1]:
        cosine = cosine * square + c
    heavy = weight * inverse
    bent = heavy * sine
    return (heavy - bent * sine).astype(BF16), (bent * cosine).astype(BF16)


def kernel(
    nw, nl, sv, se, xv, xe, pb, ab, primal_out, adjoint_out,
    slab_pad, source_pad, source_rows, slab_rows, features, areas, adjoint_pack,
    gathered, primal_acc, adjoint_send, adjoint_recv, primal_send, primal_recv,
    gather_out, gather_in, adjoint_go, adjoint_in, primal_go, primal_in,
):
    wide_at = lax.axis_index("wide")
    long_at = lax.axis_index("long")
    slab_width = se.shape[1]
    source_width = xe.shape[1]
    blocks = slab_width // 128

    barrier = pltpu.get_barrier_semaphore()

    def greet_wide(k, carry):
        pl.semaphore_signal(
            barrier, inc=1, device_id=(lax.rem(wide_at + k, nw), long_at), device_id_type=MESH
        )
        return carry

    def greet_long(k, carry):
        pl.semaphore_signal(
            barrier, inc=1, device_id=(wide_at, lax.rem(long_at + k, nl)), device_id_type=MESH
        )
        return carry

    lax.fori_loop(1, nw, greet_wide, 0)
    lax.fori_loop(1, nl, greet_long, 0)

    source_pad[...] = jnp.zeros_like(source_pad)
    source_pad[0:3, :] = xv[...]
    anchor = (wide_at * nl + long_at) * (source_width // 2)
    centre, area, norm = points(source_pad[...], xe[...], anchor)
    for n, piece in enumerate(split3(centre * (-2.0 * SCALE))):
        source_rows[3 * n : 3 * n + 3, :] = piece[0:3]
    for n, piece in enumerate(split3(SCALE * (norm + AREA_WEIGHT * area))):
        source_rows[9 + n : 10 + n, :] = piece
    source_rows[12:13, :] = jnp.ones((1, source_width), F32)
    for n, piece in enumerate(split3(area)):
        source_rows[13 + n : 14 + n, :] = piece
    gathered[0, 0:32, :] = pb[...]
    gathered[0, 32:48, :] = source_rows[...].astype(BF16)

    pl.semaphore_wait(barrier, nw + nl - 2)

    def gather_copy(k):
        return pltpu.make_async_remote_copy(
            src_ref=gathered.at[0],
            dst_ref=gathered.at[k],
            send_sem=gather_out.at[k],
            recv_sem=gather_in.at[k],
            device_id=(lax.rem(wide_at + nw - k, nw), long_at),
            device_id_type=MESH,
        )

    def gather_start(k, carry):
        gather_copy(k).start()
        return carry

    lax.fori_loop(1, nw, gather_start, 0)

    slab_pad[...] = jnp.zeros_like(slab_pad)
    slab_pad[0:3, :] = sv[...]
    centre, area, norm = points(slab_pad[...], se[...], wide_at * (slab_width // 2))
    one, two, three = (piece[0:3] for piece in split3(centre))
    norms = split3(SCALE * (norm + SOFTENING + AREA_WEIGHT * area))
    slab_rows[...] = jnp.zeros_like(slab_rows)
    for n in range(3):
        slab_rows[3 * n : 3 * n + 3, :] = one
        slab_rows[9 + n : 10 + n, :] = jnp.ones((1, slab_width), F32)
        slab_rows[16 * n + 12 : 16 * n + 13, :] = norms[n]
    for n in range(2):
        slab_rows[16 + 3 * n : 19 + 3 * n, :] = two
    slab_rows[32:35, :] = three
    slab_rows[48:49, :] = WEIGHT * area
    turned = slab_rows[...].T
    features[...] = turned[:, 0:ROWS].astype(BF16)
    areas[...] = jnp.broadcast_to(turned[:, 48:49], areas.shape)

    rows = ab[...]
    crossed = jnp.concatenate([rows[16:32], -rows[0:16]], axis=0)
    for b in range(blocks):
        adjoint_pack[b, :, 0:128] = rows[:, 128 * b : 128 * b + 128]
        adjoint_pack[b, :, 128:256] = crossed[:, 128 * b : 128 * b + 128]
    primal_acc[...] = jnp.zeros_like(primal_acc)

    def adjoint_copy(k):
        return pltpu.make_async_remote_copy(
            src_ref=adjoint_send.at[k],
            dst_ref=adjoint_recv.at[k],
            send_sem=adjoint_go.at[k],
            recv_sem=adjoint_in.at[k],
            device_id=(lax.rem(wide_at + k, nw), long_at),
            device_id_type=MESH,
        )

    def step(k, carry):
        @pl.when(k > 0)
        def _():
            gather_copy(k).wait_recv()

        columns = gathered[k, 0:32, :]
        turned_columns = jnp.concatenate([-columns[16:32], columns[0:16]], axis=0)
        primal_pack = jnp.concatenate([columns, turned_columns], axis=1)
        source = gathered[k, 32:48, :]
        stacked = jnp.concatenate([source, source, source], axis=0)
        wide_source = source.astype(F32)
        source_area = wide_source[13:14] + wide_source[14:15] + wide_source[15:16]
        total = jnp.zeros((32, 128), F32)
        for b in range(blocks):
            distance = jnp.dot(
                features[128 * b : 128 * b + 128, :], stacked, preferred_element_type=F32
            )
            reals, imags = [], []
            for q in range(4):
                weight = areas[128 * b + 32 * q : 128 * b + 32 * q + 32, :] * source_area
                real, imag = tile_values(distance[32 * q : 32 * q + 32, :], weight)
                reals.append(real)
                imags.append(imag)
            real = jnp.concatenate(reals, axis=0)
            imag = jnp.concatenate(imags, axis=0)
            total = total + jnp.dot(
                adjoint_pack[b], jnp.concatenate([real, imag], axis=0), preferred_element_type=F32
            )
            primal_acc[:, 128 * b : 128 * b + 128] += lax.dot_general(
                primal_pack,
                jnp.concatenate([real, imag], axis=1),
                (((1,), (1,)), ((), ())),
                preferred_element_type=F32,
            )
        adjoint_send[k] = total

        @pl.when(k > 0)
        def _():
            adjoint_copy(k).start()

        return carry

    lax.fori_loop(0, nw, step, 0)

    lane = lax.broadcasted_iota(jnp.int32, (8, 128), 1) // 32
    for b in range(blocks):
        held = [primal_acc[8 * j : 8 * j + 8, 128 * b : 128 * b + 128] for j in range(4)]
        for q in range(4):
            piece = jnp.zeros((8, 128), F32)
            for j in range(4):
                shift = (32 * (j - q)) % 128
                moved = held[j] if shift == 0 else pltpu.roll(held[j], shift, 1)
                piece = jnp.where(lane == j, moved, piece)
            primal_send[4 * b + q] = piece

    def primal_copy(k):
        peer = lax.rem(long_at + k, nl)
        return pltpu.make_async_remote_copy(
            src_ref=primal_send.at[peer],
            dst_ref=primal_recv.at[k],
            send_sem=primal_go.at[k],
            recv_sem=primal_in.at[k],
            device_id=(wide_at, peer),
            device_id_type=MESH,
        )

    def primal_start(k, carry):
        primal_copy(k).start()
        return carry

    lax.fori_loop(1, nl, primal_start, 0)

    def adjoint_sum(k, total):
        adjoint_copy(k).wait_recv()
        return total + adjoint_recv[k]

    adjoint_out[...] = lax.fori_loop(1, nw, adjoint_sum, adjoint_send[0])

    def primal_sum(k, total):
        primal_copy(k).wait_recv()
        return total + primal_recv[k]

    total = lax.fori_loop(1, nl, primal_sum, primal_send[long_at])
    for j in range(4):
        primal_out[8 * j : 8 * j + 8, :] = total[:, 32 * j : 32 * j + 32]

    def finish_wide(k, carry):
        gather_copy(k).wait_send()
        adjoint_copy(k).wait_send()
        return carry

    def finish_long(k, carry):
        primal_copy(k).wait_send()
        return carry

    lax.fori_loop(1, nw, finish_wide, 0)
    lax.fori_loop(1, nl, finish_long, 0)


def solution(mesh):
    nw, nl = mesh.shape["wide"], mesh.shape["long"]

    def shards(sv, se, xv, xe, pb, ab):
        slab_width, source_width = se.shape[1], xe.shape[1]
        vmem = pl.BlockSpec(memory_space=pltpu.VMEM)
        return pl.pallas_call(
            functools.partial(kernel, nw, nl),
            out_shape=(
                jax.ShapeDtypeStruct((32, slab_width // nl), F32),
                jax.ShapeDtypeStruct((32, source_width), F32),
            ),
            in_specs=[vmem] * 6,
            out_specs=(vmem, vmem),
            scratch_shapes=[
                pltpu.VMEM((8, sv.shape[1]), F32),
                pltpu.VMEM((8, xv.shape[1]), F32),
                pltpu.VMEM((16, source_width), F32),
                pltpu.VMEM((64, slab_width), F32),
                pltpu.VMEM((slab_width, ROWS), BF16),
                pltpu.VMEM((slab_width, 128), F32),
                pltpu.VMEM((slab_width // 128, 32, 256), BF16),
                pltpu.VMEM((nw, ROWS, source_width), BF16),
                pltpu.VMEM((32, slab_width), F32),
                pltpu.VMEM((nw, 32, source_width), F32),
                pltpu.VMEM((nw, 32, source_width), F32),
                pltpu.VMEM((nl, 8, 128), F32),
                pltpu.VMEM((nl, 8, 128), F32),
                pltpu.SemaphoreType.DMA((nw,)),
                pltpu.SemaphoreType.DMA((nw,)),
                pltpu.SemaphoreType.DMA((nw,)),
                pltpu.SemaphoreType.DMA((nw,)),
                pltpu.SemaphoreType.DMA((nl,)),
                pltpu.SemaphoreType.DMA((nl,)),
            ],
            compiler_params=pltpu.CompilerParams(collective_id=0, has_side_effects=True),
        )(sv, se, xv, xe, pb, ab)

    return jax.shard_map(
        shards,
        mesh=mesh,
        in_specs=(
            P(None, "wide"),
            P(None, "wide"),
            P(None, ("wide", "long")),
            P(None, ("wide", "long")),
            P(None, ("wide", "long")),
            P(None, "wide"),
        ),
        out_specs=(P(None, ("wide", "long")), P(None, ("wide", "long"))),
        check_vma=False,
    )
```

```python
import functools
import math

import jax
import jax.numpy as jnp
from jax import lax
from jax.experimental import pallas as pl
from jax.experimental.pallas import tpu as pltpu
from jax.sharding import PartitionSpec as P

WAVENUMBER = 40.0
SOFTENING = 0.0004
AREA_WEIGHT = 0.05
TURNS = WAVENUMBER / (2.0 * math.pi)
SCALE = TURNS * TURNS
WEIGHT = TURNS / (4.0 * math.pi)
ROUND = 12582912.0
ROOT2 = math.sqrt(2.0)
SIN = tuple(ROOT2 * c for c in (3.14158202, -5.16714279, 2.54189895, -0.55463599))
COS = tuple(ROOT2 * c for c in (0.99999995, -4.93479286, 4.05841191, -1.33188013, 0.21969673))
ROWS = 48
GROUP = 3
PIECE = 32
MESH = pl.DeviceIdType.MESH
F32 = jnp.float32
BF16 = jnp.bfloat16


def split3(x):
    one = x.astype(BF16).astype(F32)
    rest = x - one
    two = rest.astype(BF16).astype(F32)
    three = (rest - two).astype(BF16).astype(F32)
    return one, two, three


def points(padded, ids, anchor):
    count, width = padded.shape[1], ids.shape[1]
    parts = jnp.concatenate(split3(padded), axis=0).astype(BF16)
    rows = lax.broadcasted_iota(jnp.int32, (count, width), 0) + anchor
    corners = []
    for corner in range(3):
        chosen = jnp.where(rows == ids[corner : corner + 1, :], 1.0, 0.0).astype(BF16)
        found = jnp.dot(parts, chosen, preferred_element_type=F32)
        corners.append(found[0:8] + found[8:16] + found[16:24])
    centre = (corners[0] + corners[1] + corners[2]) * (1.0 / 3.0) - 0.5
    one = corners[1] - corners[0]
    two = corners[2] - corners[0]
    ox, oy, oz = one[0:1], one[1:2], one[2:3]
    tx, ty, tz = two[0:1], two[1:2], two[2:3]
    nx = oy * tz - oz * ty
    ny = oz * tx - ox * tz
    nz = ox * ty - oy * tx
    area = 0.5 * jnp.sqrt(nx * nx + ny * ny + nz * nz)
    square = centre * centre
    norm = square[0:1] + square[1:2] + square[2:3]
    return centre, area, norm


def tile_values(scaled, weight):
    inverse = lax.rsqrt(scaled)
    turns = scaled * inverse
    part = turns - ((turns + ROUND) - ROUND)
    square = part * part
    sine = SIN[3]
    for c in SIN[2::-1]:
        sine = sine * square + c
    sine = sine * part
    cosine = COS[4]
    for c in COS[3::-1]:
        cosine = cosine * square + c
    heavy = weight * inverse
    bent = heavy * sine
    return (heavy - bent * sine).astype(BF16), (bent * cosine).astype(BF16)


def kernel(
    nw, nl, sv, se, xv, xe, pb, ab, primal_out, adjoint_out,
    slab_pad, source_pad, source_rows, slab_rows, features, areas, adjoint_pack,
    gathered, primal_acc, adjoint_send, adjoint_recv, primal_send, primal_recv,
    gather_out, gather_in, adjoint_go, adjoint_in, primal_go, primal_in,
):
    wide_at = lax.axis_index("wide")
    long_at = lax.axis_index("long")
    slab_width = se.shape[1]
    source_width = xe.shape[1]
    blocks = slab_width // 128

    barrier = pltpu.get_barrier_semaphore()

    def greet_wide(k, carry):
        pl.semaphore_signal(
            barrier, inc=1, device_id=(lax.rem(wide_at + k, nw), long_at), device_id_type=MESH
        )
        return carry

    def greet_long(k, carry):
        pl.semaphore_signal(
            barrier, inc=1, device_id=(wide_at, lax.rem(long_at + k, nl)), device_id_type=MESH
        )
        return carry

    lax.fori_loop(1, nw, greet_wide, 0)
    lax.fori_loop(1, nl, greet_long, 0)

    source_pad[...] = jnp.zeros_like(source_pad)
    source_pad[0:3, :] = xv[...]
    anchor = (wide_at * nl + long_at) * (source_width // 2)
    centre, area, norm = points(source_pad[...], xe[...], anchor)
    for n, piece in enumerate(split3(centre * (-2.0 * SCALE))):
        source_rows[3 * n : 3 * n + 3, :] = piece[0:3]
    for n, piece in enumerate(split3(SCALE * (norm + AREA_WEIGHT * area))):
        source_rows[9 + n : 10 + n, :] = piece
    source_rows[12:13, :] = jnp.ones((1, source_width), F32)
    for n, piece in enumerate(split3(area)):
        source_rows[13 + n : 14 + n, :] = piece
    gathered[0, 0:32, :] = pb[...]
    gathered[0, 32:48, :] = source_rows[...].astype(BF16)

    pl.semaphore_wait(barrier, nw + nl - 2)

    def gather_copy(k):
        return pltpu.make_async_remote_copy(
            src_ref=gathered.at[0],
            dst_ref=gathered.at[k],
            send_sem=gather_out.at[k],
            recv_sem=gather_in.at[k],
            device_id=(lax.rem(wide_at + nw - k, nw), long_at),
            device_id_type=MESH,
        )

    def gather_start(k, carry):
        gather_copy(k).start()
        return carry

    lax.fori_loop(1, nw, gather_start, 0)

    slab_pad[...] = jnp.zeros_like(slab_pad)
    slab_pad[0:3, :] = sv[...]
    centre, area, norm = points(slab_pad[...], se[...], wide_at * (slab_width // 2))
    one, two, three = (piece[0:3] for piece in split3(centre))
    norms = split3(SCALE * (norm + SOFTENING + AREA_WEIGHT * area))
    slab_rows[...] = jnp.zeros_like(slab_rows)
    for n in range(3):
        slab_rows[3 * n : 3 * n + 3, :] = one
        slab_rows[9 + n : 10 + n, :] = jnp.ones((1, slab_width), F32)
        slab_rows[16 * n + 12 : 16 * n + 13, :] = norms[n]
    for n in range(2):
        slab_rows[16 + 3 * n : 19 + 3 * n, :] = two
    slab_rows[32:35, :] = three
    slab_rows[48:49, :] = WEIGHT * area
    turned = slab_rows[...].T
    features[...] = turned[:, 0:ROWS].astype(BF16)
    areas[...] = jnp.broadcast_to(turned[:, 48:49], areas.shape)

    rows = ab[...]
    crossed = jnp.concatenate([rows[16:32], -rows[0:16]], axis=0)
    for b in range(blocks):
        adjoint_pack[b, :, 0:128] = rows[:, 128 * b : 128 * b + 128]
        adjoint_pack[b, :, 128:256] = crossed[:, 128 * b : 128 * b + 128]
    primal_acc[...] = jnp.zeros_like(primal_acc)

    def adjoint_copy(k):
        return pltpu.make_async_remote_copy(
            src_ref=adjoint_send.at[k],
            dst_ref=adjoint_recv.at[k],
            send_sem=adjoint_go.at[k],
            recv_sem=adjoint_in.at[k],
            device_id=(lax.rem(wide_at + k, nw), long_at),
            device_id_type=MESH,
        )

    def distances(k, b):
        source = gathered[k, 32:48, :]
        stacked = jnp.concatenate([source, source, source], axis=0)
        return jnp.dot(
            features[128 * b : 128 * b + 128, :], stacked, preferred_element_type=F32
        )

    def values(k, b, distance):
        source = gathered[k, 32:48, :].astype(F32)
        source_area = source[13:14] + source[14:15] + source[15:16]
        reals, imags = [], []
        for q in range(128 // PIECE):
            at = 128 * b + PIECE * q
            weight = areas[at : at + PIECE, :] * source_area
            real, imag = tile_values(distance[PIECE * q : PIECE * q + PIECE, :], weight)
            reals.append(real)
            imags.append(imag)
        return jnp.concatenate(reals, axis=0), jnp.concatenate(imags, axis=0)

    def images(k, b, real, imag):
        columns = gathered[k, 0:32, :]
        turned_columns = jnp.concatenate([-columns[16:32], columns[0:16]], axis=0)
        primal_acc[:, 128 * b : 128 * b + 128] += lax.dot_general(
            jnp.concatenate([columns, turned_columns], axis=1),
            jnp.concatenate([real, imag], axis=1),
            (((1,), (1,)), ((), ())),
            preferred_element_type=F32,
        )
        return jnp.dot(
            adjoint_pack[b], jnp.concatenate([real, imag], axis=0), preferred_element_type=F32
        )

    def process(chunks):
        todo = [(c, b) for c in range(len(chunks)) for b in range(blocks)]
        totals = [jnp.zeros((32, 128), F32) for _ in chunks]
        ahead = distances(chunks[0], 0)
        behind = None
        for n, (c, b) in enumerate(todo):
            distance = ahead
            if n + 1 < len(todo):
                after, next_block = todo[n + 1]
                ahead = distances(chunks[after], next_block)
            if behind is not None:
                old, old_block, pair = behind
                totals[old] = totals[old] + images(chunks[old], old_block, *pair)
            behind = (c, b, values(chunks[c], b, distance))
        old, old_block, pair = behind
        totals[old] = totals[old] + images(chunks[old], old_block, *pair)
        for c, k in enumerate(chunks):
            adjoint_send[k] = totals[c]

    def step(g, carry):
        first = 1 + g * GROUP

        for c in range(GROUP):
            gather_copy(first + c).wait_recv()
        process([first + c for c in range(GROUP)])
        for c in range(GROUP):
            adjoint_copy(first + c).start()
        return carry

    process([0])
    lax.fori_loop(0, (nw - 1) // GROUP, step, 0)

    lane = lax.broadcasted_iota(jnp.int32, (8, 128), 1) // 32
    for b in range(blocks):
        held = [primal_acc[8 * j : 8 * j + 8, 128 * b : 128 * b + 128] for j in range(4)]
        for q in range(4):
            piece = jnp.zeros((8, 128), F32)
            for j in range(4):
                shift = (32 * (j - q)) % 128
                moved = held[j] if shift == 0 else pltpu.roll(held[j], shift, 1)
                piece = jnp.where(lane == j, moved, piece)
            primal_send[4 * b + q] = piece

    def primal_copy(k):
        peer = lax.rem(long_at + k, nl)
        return pltpu.make_async_remote_copy(
            src_ref=primal_send.at[peer],
            dst_ref=primal_recv.at[k],
            send_sem=primal_go.at[k],
            recv_sem=primal_in.at[k],
            device_id=(wide_at, peer),
            device_id_type=MESH,
        )

    def primal_start(k, carry):
        primal_copy(k).start()
        return carry

    lax.fori_loop(1, nl, primal_start, 0)

    def adjoint_sum(k, total):
        adjoint_copy(k).wait_recv()
        return total + adjoint_recv[k]

    adjoint_out[...] = lax.fori_loop(1, nw, adjoint_sum, adjoint_send[0])

    def primal_sum(k, total):
        primal_copy(k).wait_recv()
        return total + primal_recv[k]

    total = lax.fori_loop(1, nl, primal_sum, primal_send[long_at])
    for j in range(4):
        primal_out[8 * j : 8 * j + 8, :] = total[:, 32 * j : 32 * j + 32]

    def finish_wide(k, carry):
        gather_copy(k).wait_send()
        adjoint_copy(k).wait_send()
        return carry

    def finish_long(k, carry):
        primal_copy(k).wait_send()
        return carry

    lax.fori_loop(1, nw, finish_wide, 0)
    lax.fori_loop(1, nl, finish_long, 0)


def solution(mesh):
    nw, nl = mesh.shape["wide"], mesh.shape["long"]

    def shards(sv, se, xv, xe, pb, ab):
        slab_width, source_width = se.shape[1], xe.shape[1]
        vmem = pl.BlockSpec(memory_space=pltpu.VMEM)
        return pl.pallas_call(
            functools.partial(kernel, nw, nl),
            out_shape=(
                jax.ShapeDtypeStruct((32, slab_width // nl), F32),
                jax.ShapeDtypeStruct((32, source_width), F32),
            ),
            in_specs=[vmem] * 6,
            out_specs=(vmem, vmem),
            scratch_shapes=[
                pltpu.VMEM((8, sv.shape[1]), F32),
                pltpu.VMEM((8, xv.shape[1]), F32),
                pltpu.VMEM((16, source_width), F32),
                pltpu.VMEM((64, slab_width), F32),
                pltpu.VMEM((slab_width, ROWS), BF16),
                pltpu.VMEM((slab_width, 128), F32),
                pltpu.VMEM((slab_width // 128, 32, 256), BF16),
                pltpu.VMEM((nw, ROWS, source_width), BF16),
                pltpu.VMEM((32, slab_width), F32),
                pltpu.VMEM((nw, 32, source_width), F32),
                pltpu.VMEM((nw, 32, source_width), F32),
                pltpu.VMEM((nl, 8, 128), F32),
                pltpu.VMEM((nl, 8, 128), F32),
                pltpu.SemaphoreType.DMA((nw,)),
                pltpu.SemaphoreType.DMA((nw,)),
                pltpu.SemaphoreType.DMA((nw,)),
                pltpu.SemaphoreType.DMA((nw,)),
                pltpu.SemaphoreType.DMA((nl,)),
                pltpu.SemaphoreType.DMA((nl,)),
            ],
            compiler_params=pltpu.CompilerParams(collective_id=0, has_side_effects=True),
        )(sv, se, xv, xe, pb, ab)

    return jax.shard_map(
        shards,
        mesh=mesh,
        in_specs=(
            P(None, "wide"),
            P(None, "wide"),
            P(None, ("wide", "long")),
            P(None, ("wide", "long")),
            P(None, ("wide", "long")),
            P(None, "wide"),
        ),
        out_specs=(P(None, ("wide", "long")), P(None, ("wide", "long"))),
        check_vma=False,
    )
```

```python
import functools
import math

import jax
import jax.numpy as jnp
from jax import lax
from jax.experimental import pallas as pl
from jax.experimental.pallas import tpu as pltpu
from jax.sharding import PartitionSpec as P

WAVENUMBER = 40.0
SOFTENING = 0.0004
AREA_WEIGHT = 0.05
TURNS = WAVENUMBER / (2.0 * math.pi)
SCALE = TURNS * TURNS
WEIGHT = TURNS / (4.0 * math.pi)
ROUND = 12582912.0
ROOT2 = math.sqrt(2.0)
SIN = tuple(ROOT2 * c for c in (3.14158202, -5.16714279, 2.54189895, -0.55463599))
COS = tuple(ROOT2 * c for c in (0.99999995, -4.93479286, 4.05841191, -1.33188013, 0.21969673))
ROWS = 48
GROUP = 3
PIECE = 32
MESH = pl.DeviceIdType.MESH
F32 = jnp.float32
BF16 = jnp.bfloat16


def split3(x):
    one = x.astype(BF16).astype(F32)
    rest = x - one
    two = rest.astype(BF16).astype(F32)
    three = (rest - two).astype(BF16).astype(F32)
    return one, two, three


def points(padded, ids, anchor):
    count, width = padded.shape[1], ids.shape[1]
    parts = jnp.concatenate(split3(padded), axis=0).astype(BF16)
    rows = lax.broadcasted_iota(jnp.int32, (count, width), 0) + anchor
    corners = []
    for corner in range(3):
        chosen = jnp.where(rows == ids[corner : corner + 1, :], 1.0, 0.0).astype(BF16)
        found = jnp.dot(parts, chosen, preferred_element_type=F32)
        corners.append(found[0:8] + found[8:16] + found[16:24])
    centre = (corners[0] + corners[1] + corners[2]) * (1.0 / 3.0) - 0.5
    one = corners[1] - corners[0]
    two = corners[2] - corners[0]
    ox, oy, oz = one[0:1], one[1:2], one[2:3]
    tx, ty, tz = two[0:1], two[1:2], two[2:3]
    nx = oy * tz - oz * ty
    ny = oz * tx - ox * tz
    nz = ox * ty - oy * tx
    area = 0.5 * jnp.sqrt(nx * nx + ny * ny + nz * nz)
    square = centre * centre
    norm = square[0:1] + square[1:2] + square[2:3]
    return centre, area, norm


def tile_values(scaled, weight):
    inverse = lax.rsqrt(scaled)
    turns = scaled * inverse
    part = turns - ((turns + ROUND) - ROUND)
    square = part * part
    sine = SIN[3]
    for c in SIN[2::-1]:
        sine = sine * square + c
    sine = sine * part
    cosine = COS[4]
    for c in COS[3::-1]:
        cosine = cosine * square + c
    heavy = weight * inverse
    bent = heavy * sine
    return (heavy - bent * sine).astype(BF16), (bent * cosine).astype(BF16)


def kernel(
    nw, nl, sv_far, se_far, xv_far, xe_far, pb_far, ab_far, primal_out, adjoint_out,
    sv, se, xv, xe, pb, ab, arrived,
    slab_pad, source_pad, source_rows, slab_rows, features, areas, adjoint_pack,
    gathered, primal_acc, adjoint_send, adjoint_recv, primal_send, primal_recv,
    gather_out, gather_in, adjoint_go, adjoint_in, primal_go, primal_in,
):
    wide_at = lax.axis_index("wide")
    long_at = lax.axis_index("long")
    slab_width = se.shape[1]
    source_width = xe.shape[1]
    blocks = slab_width // 128

    barrier = pltpu.get_barrier_semaphore()

    def greet_wide(k, carry):
        pl.semaphore_signal(
            barrier, inc=1, device_id=(lax.rem(wide_at + k, nw), long_at), device_id_type=MESH
        )
        return carry

    def greet_long(k, carry):
        pl.semaphore_signal(
            barrier, inc=1, device_id=(wide_at, lax.rem(long_at + k, nl)), device_id_type=MESH
        )
        return carry

    lax.fori_loop(1, nw, greet_wide, 0)
    lax.fori_loop(1, nl, greet_long, 0)

    fetches = [
        pltpu.make_async_copy(far, near, arrived.at[n])
        for n, (far, near) in enumerate(
            ((xv_far, xv), (xe_far, xe), (pb_far, pb), (sv_far, sv), (se_far, se), (ab_far, ab))
        )
    ]
    for fetch in fetches:
        fetch.start()

    for fetch in fetches[:3]:
        fetch.wait()
    source_pad[...] = jnp.zeros_like(source_pad)
    source_pad[0:3, :] = xv[...]
    anchor = (wide_at * nl + long_at) * (source_width // 2)
    centre, area, norm = points(source_pad[...], xe[...], anchor)
    for n, piece in enumerate(split3(centre * (-2.0 * SCALE))):
        source_rows[3 * n : 3 * n + 3, :] = piece[0:3]
    for n, piece in enumerate(split3(SCALE * (norm + AREA_WEIGHT * area))):
        source_rows[9 + n : 10 + n, :] = piece
    source_rows[12:13, :] = jnp.ones((1, source_width), F32)
    for n, piece in enumerate(split3(area)):
        source_rows[13 + n : 14 + n, :] = piece
    gathered[0, 0:32, :] = pb[...]
    gathered[0, 32:48, :] = source_rows[...].astype(BF16)

    pl.semaphore_wait(barrier, nw + nl - 2)

    def gather_copy(k):
        return pltpu.make_async_remote_copy(
            src_ref=gathered.at[0],
            dst_ref=gathered.at[k],
            send_sem=gather_out.at[k],
            recv_sem=gather_in.at[k],
            device_id=(lax.rem(wide_at + nw - k, nw), long_at),
            device_id_type=MESH,
        )

    def gather_start(k, carry):
        gather_copy(k).start()
        return carry

    lax.fori_loop(1, nw, gather_start, 0)

    for fetch in fetches[3:]:
        fetch.wait()
    slab_pad[...] = jnp.zeros_like(slab_pad)
    slab_pad[0:3, :] = sv[...]
    centre, area, norm = points(slab_pad[...], se[...], wide_at * (slab_width // 2))
    one, two, three = (piece[0:3] for piece in split3(centre))
    norms = split3(SCALE * (norm + SOFTENING + AREA_WEIGHT * area))
    slab_rows[...] = jnp.zeros_like(slab_rows)
    for n in range(3):
        slab_rows[3 * n : 3 * n + 3, :] = one
        slab_rows[9 + n : 10 + n, :] = jnp.ones((1, slab_width), F32)
        slab_rows[16 * n + 12 : 16 * n + 13, :] = norms[n]
    for n in range(2):
        slab_rows[16 + 3 * n : 19 + 3 * n, :] = two
    slab_rows[32:35, :] = three
    slab_rows[48:49, :] = WEIGHT * area
    turned = slab_rows[...].T
    features[...] = turned[:, 0:ROWS].astype(BF16)
    areas[...] = jnp.broadcast_to(turned[:, 48:49], areas.shape)

    rows = ab[...]
    crossed = jnp.concatenate([rows[16:32], -rows[0:16]], axis=0)
    for b in range(blocks):
        adjoint_pack[b, :, 0:128] = rows[:, 128 * b : 128 * b + 128]
        adjoint_pack[b, :, 128:256] = crossed[:, 128 * b : 128 * b + 128]
    primal_acc[...] = jnp.zeros_like(primal_acc)

    def adjoint_copy(k):
        return pltpu.make_async_remote_copy(
            src_ref=adjoint_send.at[k],
            dst_ref=adjoint_recv.at[k],
            send_sem=adjoint_go.at[k],
            recv_sem=adjoint_in.at[k],
            device_id=(lax.rem(wide_at + k, nw), long_at),
            device_id_type=MESH,
        )

    def distances(k, b):
        source = gathered[k, 32:48, :]
        stacked = jnp.concatenate([source, source, source], axis=0)
        return jnp.dot(
            features[128 * b : 128 * b + 128, :], stacked, preferred_element_type=F32
        )

    def values(k, b, distance):
        source = gathered[k, 32:48, :].astype(F32)
        source_area = source[13:14] + source[14:15] + source[15:16]
        reals, imags = [], []
        for q in range(128 // PIECE):
            at = 128 * b + PIECE * q
            weight = areas[at : at + PIECE, :] * source_area
            real, imag = tile_values(distance[PIECE * q : PIECE * q + PIECE, :], weight)
            reals.append(real)
            imags.append(imag)
        return jnp.concatenate(reals, axis=0), jnp.concatenate(imags, axis=0)

    def images(k, b, real, imag):
        columns = gathered[k, 0:32, :]
        turned_columns = jnp.concatenate([-columns[16:32], columns[0:16]], axis=0)
        primal_acc[:, 128 * b : 128 * b + 128] += lax.dot_general(
            jnp.concatenate([columns, turned_columns], axis=1),
            jnp.concatenate([real, imag], axis=1),
            (((1,), (1,)), ((), ())),
            preferred_element_type=F32,
        )
        return jnp.dot(
            adjoint_pack[b], jnp.concatenate([real, imag], axis=0), preferred_element_type=F32
        )

    def process(chunks):
        todo = [(c, b) for c in range(len(chunks)) for b in range(blocks)]
        totals = [jnp.zeros((32, 128), F32) for _ in chunks]
        ahead = distances(chunks[0], 0)
        behind = None
        for n, (c, b) in enumerate(todo):
            distance = ahead
            if n + 1 < len(todo):
                after, next_block = todo[n + 1]
                ahead = distances(chunks[after], next_block)
            if behind is not None:
                old, old_block, pair = behind
                totals[old] = totals[old] + images(chunks[old], old_block, *pair)
            behind = (c, b, values(chunks[c], b, distance))
        old, old_block, pair = behind
        totals[old] = totals[old] + images(chunks[old], old_block, *pair)
        for c, k in enumerate(chunks):
            adjoint_send[k] = totals[c]

    def step(g, carry):
        first = 1 + g * GROUP

        for c in range(GROUP):
            gather_copy(first + c).wait_recv()
        process([first + c for c in range(GROUP)])
        for c in range(GROUP):
            adjoint_copy(first + c).start()
        return carry

    process([0])
    lax.fori_loop(0, (nw - 1) // GROUP, step, 0)

    lane = lax.broadcasted_iota(jnp.int32, (8, 128), 1) // 32
    for b in range(blocks):
        held = [primal_acc[8 * j : 8 * j + 8, 128 * b : 128 * b + 128] for j in range(4)]
        for q in range(4):
            piece = jnp.zeros((8, 128), F32)
            for j in range(4):
                shift = (32 * (j - q)) % 128
                moved = held[j] if shift == 0 else pltpu.roll(held[j], shift, 1)
                piece = jnp.where(lane == j, moved, piece)
            primal_send[4 * b + q] = piece

    def primal_copy(k):
        peer = lax.rem(long_at + k, nl)
        return pltpu.make_async_remote_copy(
            src_ref=primal_send.at[peer],
            dst_ref=primal_recv.at[k],
            send_sem=primal_go.at[k],
            recv_sem=primal_in.at[k],
            device_id=(wide_at, peer),
            device_id_type=MESH,
        )

    def primal_start(k, carry):
        primal_copy(k).start()
        return carry

    lax.fori_loop(1, nl, primal_start, 0)

    def adjoint_sum(k, total):
        adjoint_copy(k).wait_recv()
        return total + adjoint_recv[k]

    adjoint_out[...] = lax.fori_loop(1, nw, adjoint_sum, adjoint_send[0])

    def primal_sum(k, total):
        primal_copy(k).wait_recv()
        return total + primal_recv[k]

    total = lax.fori_loop(1, nl, primal_sum, primal_send[long_at])
    for j in range(4):
        primal_out[8 * j : 8 * j + 8, :] = total[:, 32 * j : 32 * j + 32]

    def finish_wide(k, carry):
        gather_copy(k).wait_send()
        adjoint_copy(k).wait_send()
        return carry

    def finish_long(k, carry):
        primal_copy(k).wait_send()
        return carry

    lax.fori_loop(1, nw, finish_wide, 0)
    lax.fori_loop(1, nl, finish_long, 0)


def write_out(primal, adjoint, primal_out, adjoint_out, done):
    one = pltpu.make_async_copy(primal, primal_out, done.at[0])
    two = pltpu.make_async_copy(adjoint, adjoint_out, done.at[1])
    one.start()
    two.start()
    one.wait()
    two.wait()


def solution(mesh):
    nw, nl = mesh.shape["wide"], mesh.shape["long"]

    def shards(sv, se, xv, xe, pb, ab):
        slab_width, source_width = se.shape[1], xe.shape[1]
        far = pl.BlockSpec(memory_space=pl.ANY)
        vmem = pl.BlockSpec(memory_space=pltpu.VMEM)
        primal, adjoint = pl.pallas_call(
            functools.partial(kernel, nw, nl),
            out_shape=(
                pltpu.VMEM((32, slab_width // nl), F32),
                pltpu.VMEM((32, source_width), F32),
            ),
            in_specs=[far] * 6,
            out_specs=(vmem, vmem),
            scratch_shapes=[
                *(pltpu.VMEM(x.shape, x.dtype) for x in (sv, se, xv, xe, pb, ab)),
                pltpu.SemaphoreType.DMA((6,)),
                pltpu.VMEM((8, sv.shape[1]), F32),
                pltpu.VMEM((8, xv.shape[1]), F32),
                pltpu.VMEM((16, source_width), F32),
                pltpu.VMEM((64, slab_width), F32),
                pltpu.VMEM((slab_width, ROWS), BF16),
                pltpu.VMEM((slab_width, 128), F32),
                pltpu.VMEM((slab_width // 128, 32, 256), BF16),
                pltpu.VMEM((nw, ROWS, source_width), BF16),
                pltpu.VMEM((32, slab_width), F32),
                pltpu.VMEM((nw, 32, source_width), F32),
                pltpu.VMEM((nw, 32, source_width), F32),
                pltpu.VMEM((nl, 8, 128), F32),
                pltpu.VMEM((nl, 8, 128), F32),
                pltpu.SemaphoreType.DMA((nw,)),
                pltpu.SemaphoreType.DMA((nw,)),
                pltpu.SemaphoreType.DMA((nw,)),
                pltpu.SemaphoreType.DMA((nw,)),
                pltpu.SemaphoreType.DMA((nl,)),
                pltpu.SemaphoreType.DMA((nl,)),
            ],
            compiler_params=pltpu.CompilerParams(collective_id=0, has_side_effects=True),
        )(sv, se, xv, xe, pb, ab)
        return pl.pallas_call(
            write_out,
            out_shape=(
                jax.ShapeDtypeStruct(primal.shape, F32),
                jax.ShapeDtypeStruct(adjoint.shape, F32),
            ),
            in_specs=[vmem, vmem],
            out_specs=(far, far),
            scratch_shapes=[pltpu.SemaphoreType.DMA((2,))],
        )(
            pltpu.with_memory_space_constraint(primal, pltpu.VMEM),
            pltpu.with_memory_space_constraint(adjoint, pltpu.VMEM),
        )

    return jax.shard_map(
        shards,
        mesh=mesh,
        in_specs=(
            P(None, "wide"),
            P(None, "wide"),
            P(None, ("wide", "long")),
            P(None, ("wide", "long")),
            P(None, ("wide", "long")),
            P(None, "wide"),
        ),
        out_specs=(P(None, ("wide", "long")), P(None, ("wide", "long"))),
        check_vma=False,
    )
```

```python
import functools
import math

import jax
import jax.numpy as jnp
from jax import lax
from jax.experimental import pallas as pl
from jax.experimental.pallas import tpu as pltpu
from jax.sharding import PartitionSpec as P

WAVENUMBER = 40.0
SOFTENING = 0.0004
AREA_WEIGHT = 0.05
TURNS = WAVENUMBER / (2.0 * math.pi)
SCALE = TURNS * TURNS
WEIGHT = TURNS / (4.0 * math.pi)
ROUND = 12582912.0
ROOT2 = math.sqrt(2.0)
SIN = tuple(ROOT2 * c for c in (3.14158202, -5.16714279, 2.54189895, -0.55463599))
COS = tuple(ROOT2 * c for c in (0.99999995, -4.93479286, 4.05841191, -1.33188013, 0.21969673))
ROWS = 48
GROUP = 3
PIECE = 32
MESH = pl.DeviceIdType.MESH
F32 = jnp.float32
BF16 = jnp.bfloat16


def split3(x):
    one = x.astype(BF16).astype(F32)
    rest = x - one
    two = rest.astype(BF16).astype(F32)
    three = (rest - two).astype(BF16).astype(F32)
    return one, two, three


def points(padded, ids, anchor):
    count, width = padded.shape[1], ids.shape[1]
    parts = jnp.concatenate(split3(padded), axis=0).astype(BF16)
    rows = lax.broadcasted_iota(jnp.int32, (count, width), 0) + anchor
    corners = []
    for corner in range(3):
        chosen = jnp.where(rows == ids[corner : corner + 1, :], 1.0, 0.0).astype(BF16)
        found = jnp.dot(parts, chosen, preferred_element_type=F32)
        corners.append(found[0:8] + found[8:16] + found[16:24])
    centre = (corners[0] + corners[1] + corners[2]) * (1.0 / 3.0) - 0.5
    one = corners[1] - corners[0]
    two = corners[2] - corners[0]
    ox, oy, oz = one[0:1], one[1:2], one[2:3]
    tx, ty, tz = two[0:1], two[1:2], two[2:3]
    nx = oy * tz - oz * ty
    ny = oz * tx - ox * tz
    nz = ox * ty - oy * tx
    area = 0.5 * jnp.sqrt(nx * nx + ny * ny + nz * nz)
    square = centre * centre
    norm = square[0:1] + square[1:2] + square[2:3]
    return centre, area, norm


def tile_values(scaled, weight):
    inverse = lax.rsqrt(scaled)
    turns = scaled * inverse
    part = turns - ((turns + ROUND) - ROUND)
    square = part * part
    sine = SIN[3]
    for c in SIN[2::-1]:
        sine = sine * square + c
    sine = sine * part
    cosine = COS[4]
    for c in COS[3::-1]:
        cosine = cosine * square + c
    heavy = weight * inverse
    bent = heavy * sine
    return (heavy - bent * sine).astype(BF16), (bent * cosine).astype(BF16)


def kernel(
    nw, nl, sv_far, se_far, xv_far, xe_far, pb_far, ab_far, primal_out, adjoint_out,
    sv, se, xv, xe, pb, ab, arrived,
    slab_pad, source_pad, source_rows, slab_rows, features, areas, adjoint_pack,
    gathered, primal_acc, adjoint_send, adjoint_recv, primal_send, primal_recv,
    gather_out, gather_in, adjoint_go, adjoint_in, primal_go, primal_in, known_y, known_z, known_all,
):
    wide_at = lax.axis_index("wide")
    long_at = lax.axis_index("long")
    slab_width = se.shape[1]
    source_width = xe.shape[1]
    blocks = slab_width // 128

    barrier = pltpu.get_barrier_semaphore()

    def greet_wide(k, carry):
        pl.semaphore_signal(
            barrier, inc=1, device_id=(lax.rem(wide_at + k, nw), long_at), device_id_type=MESH
        )
        return carry

    def beside(step, size, by):
        place = (long_at // step) % size
        return long_at + ((place + by) % size - place) * step

    def greet_ring(semaphore, step):
        for by in (1, 3):
            pl.semaphore_signal(
                semaphore, inc=1, device_id=(wide_at, beside(step, 4, by)), device_id_type=MESH
            )

    lax.fori_loop(1, nw, greet_wide, 0)
    greet_ring(barrier, 4)
    greet_ring(barrier, 1)

    fetches = [
        pltpu.make_async_copy(far, near, arrived.at[n])
        for n, (far, near) in enumerate(
            ((xv_far, xv), (xe_far, xe), (pb_far, pb), (sv_far, sv), (se_far, se), (ab_far, ab))
        )
    ]
    for fetch in fetches:
        fetch.start()

    for fetch in fetches[:3]:
        fetch.wait()
    source_pad[...] = jnp.zeros_like(source_pad)
    source_pad[0:3, :] = xv[...]
    anchor = (wide_at * nl + long_at) * (source_width // 2)
    centre, area, norm = points(source_pad[...], xe[...], anchor)
    for n, piece in enumerate(split3(centre * (-2.0 * SCALE))):
        source_rows[3 * n : 3 * n + 3, :] = piece[0:3]
    for n, piece in enumerate(split3(SCALE * (norm + AREA_WEIGHT * area))):
        source_rows[9 + n : 10 + n, :] = piece
    source_rows[12:13, :] = jnp.ones((1, source_width), F32)
    for n, piece in enumerate(split3(area)):
        source_rows[13 + n : 14 + n, :] = piece
    gathered[0, 0:32, :] = pb[...]
    gathered[0, 32:48, :] = source_rows[...].astype(BF16)

    pl.semaphore_wait(barrier, nw - 1 + 4)

    def gather_copy(k):
        return pltpu.make_async_remote_copy(
            src_ref=gathered.at[0],
            dst_ref=gathered.at[k],
            send_sem=gather_out.at[k],
            recv_sem=gather_in.at[k],
            device_id=(lax.rem(wide_at + nw - k, nw), long_at),
            device_id_type=MESH,
        )

    def gather_start(k, carry):
        gather_copy(k).start()
        return carry

    lax.fori_loop(1, nw, gather_start, 0)
    greet_ring(known_y, 4)

    for fetch in fetches[3:]:
        fetch.wait()
    slab_pad[...] = jnp.zeros_like(slab_pad)
    slab_pad[0:3, :] = sv[...]
    centre, area, norm = points(slab_pad[...], se[...], wide_at * (slab_width // 2))
    one, two, three = (piece[0:3] for piece in split3(centre))
    norms = split3(SCALE * (norm + SOFTENING + AREA_WEIGHT * area))
    slab_rows[...] = jnp.zeros_like(slab_rows)
    for n in range(3):
        slab_rows[3 * n : 3 * n + 3, :] = one
        slab_rows[9 + n : 10 + n, :] = jnp.ones((1, slab_width), F32)
        slab_rows[16 * n + 12 : 16 * n + 13, :] = norms[n]
    for n in range(2):
        slab_rows[16 + 3 * n : 19 + 3 * n, :] = two
    slab_rows[32:35, :] = three
    slab_rows[48:49, :] = WEIGHT * area
    turned = slab_rows[...].T
    features[...] = turned[:, 0:ROWS].astype(BF16)
    areas[...] = jnp.broadcast_to(turned[:, 48:49], areas.shape)

    rows = ab[...]
    crossed = jnp.concatenate([rows[16:32], -rows[0:16]], axis=0)
    for b in range(blocks):
        adjoint_pack[b, :, 0:128] = rows[:, 128 * b : 128 * b + 128]
        adjoint_pack[b, :, 128:256] = crossed[:, 128 * b : 128 * b + 128]
    primal_acc[...] = jnp.zeros_like(primal_acc)

    def adjoint_copy(k):
        return pltpu.make_async_remote_copy(
            src_ref=adjoint_send.at[k],
            dst_ref=adjoint_recv.at[k],
            send_sem=adjoint_go.at[k],
            recv_sem=adjoint_in.at[k],
            device_id=(lax.rem(wide_at + k, nw), long_at),
            device_id_type=MESH,
        )

    def distances(k, b):
        source = gathered[k, 32:48, :]
        stacked = jnp.concatenate([source, source, source], axis=0)
        return jnp.dot(
            features[128 * b : 128 * b + 128, :], stacked, preferred_element_type=F32
        )

    def values(k, b, distance):
        source = gathered[k, 32:48, :].astype(F32)
        source_area = source[13:14] + source[14:15] + source[15:16]
        reals, imags = [], []
        for q in range(128 // PIECE):
            at = 128 * b + PIECE * q
            weight = areas[at : at + PIECE, :] * source_area
            real, imag = tile_values(distance[PIECE * q : PIECE * q + PIECE, :], weight)
            reals.append(real)
            imags.append(imag)
        return jnp.concatenate(reals, axis=0), jnp.concatenate(imags, axis=0)

    def images(k, b, real, imag):
        columns = gathered[k, 0:32, :]
        turned_columns = jnp.concatenate([-columns[16:32], columns[0:16]], axis=0)
        primal_acc[:, 128 * b : 128 * b + 128] += lax.dot_general(
            jnp.concatenate([columns, turned_columns], axis=1),
            jnp.concatenate([real, imag], axis=1),
            (((1,), (1,)), ((), ())),
            preferred_element_type=F32,
        )
        return jnp.dot(
            adjoint_pack[b], jnp.concatenate([real, imag], axis=0), preferred_element_type=F32
        )

    def process(chunks):
        todo = [(c, b) for c in range(len(chunks)) for b in range(blocks)]
        totals = [jnp.zeros((32, 128), F32) for _ in chunks]
        ahead = distances(chunks[0], 0)
        behind = None
        for n, (c, b) in enumerate(todo):
            distance = ahead
            if n + 1 < len(todo):
                after, next_block = todo[n + 1]
                ahead = distances(chunks[after], next_block)
            if behind is not None:
                old, old_block, pair = behind
                totals[old] = totals[old] + images(chunks[old], old_block, *pair)
            behind = (c, b, values(chunks[c], b, distance))
        old, old_block, pair = behind
        totals[old] = totals[old] + images(chunks[old], old_block, *pair)
        for c, k in enumerate(chunks):
            adjoint_send[k] = totals[c]

    def step(g, carry):
        first = 1 + g * GROUP

        for c in range(GROUP):
            gather_copy(first + c).wait_recv()
        process([first + c for c in range(GROUP)])
        for c in range(GROUP):
            adjoint_copy(first + c).start()

        @pl.when(g == 0)
        def _():
            pl.semaphore_wait(known_y, 2)
            greet_ring(known_z, 1)

        @pl.when(g == 2)
        def _():
            pl.semaphore_wait(known_z, 2)
            greet_ring(known_all, 1)

        return carry

    process([0])
    lax.fori_loop(0, (nw - 1) // GROUP, step, 0)

    pl.semaphore_wait(known_all, 2)

    lane = lax.broadcasted_iota(jnp.int32, (8, 128), 1) // 32
    for b in range(blocks):
        held = [primal_acc[8 * j : 8 * j + 8, 128 * b : 128 * b + 128] for j in range(4)]
        for q in range(4):
            piece = jnp.zeros((8, 128), F32)
            for j in range(4):
                shift = (32 * (j - q)) % 128
                moved = held[j] if shift == 0 else pltpu.roll(held[j], shift, 1)
                piece = jnp.where(lane == j, moved, piece)
            primal_send[4 * b + q] = piece

    def primal_copy(k):
        peer = lax.rem(long_at + k, nl)
        return pltpu.make_async_remote_copy(
            src_ref=primal_send.at[peer],
            dst_ref=primal_recv.at[k],
            send_sem=primal_go.at[k],
            recv_sem=primal_in.at[k],
            device_id=(wide_at, peer),
            device_id_type=MESH,
        )

    def primal_start(k, carry):
        primal_copy(k).start()
        return carry

    lax.fori_loop(1, nl, primal_start, 0)

    def adjoint_sum(k, total):
        adjoint_copy(k).wait_recv()
        return total + adjoint_recv[k]

    adjoint_out[...] = lax.fori_loop(1, nw, adjoint_sum, adjoint_send[0])

    def primal_sum(k, total):
        primal_copy(k).wait_recv()
        return total + primal_recv[k]

    total = lax.fori_loop(1, nl, primal_sum, primal_send[long_at])
    for j in range(4):
        primal_out[8 * j : 8 * j + 8, :] = total[:, 32 * j : 32 * j + 32]

    def finish_wide(k, carry):
        gather_copy(k).wait_send()
        adjoint_copy(k).wait_send()
        return carry

    def finish_long(k, carry):
        primal_copy(k).wait_send()
        return carry

    lax.fori_loop(1, nw, finish_wide, 0)
    lax.fori_loop(1, nl, finish_long, 0)


def write_out(primal, adjoint, primal_out, adjoint_out, done):
    one = pltpu.make_async_copy(primal, primal_out, done.at[0])
    two = pltpu.make_async_copy(adjoint, adjoint_out, done.at[1])
    one.start()
    two.start()
    one.wait()
    two.wait()


def solution(mesh):
    nw, nl = mesh.shape["wide"], mesh.shape["long"]

    def shards(sv, se, xv, xe, pb, ab):
        slab_width, source_width = se.shape[1], xe.shape[1]
        far = pl.BlockSpec(memory_space=pl.ANY)
        vmem = pl.BlockSpec(memory_space=pltpu.VMEM)
        primal, adjoint = pl.pallas_call(
            functools.partial(kernel, nw, nl),
            out_shape=(
                pltpu.VMEM((32, slab_width // nl), F32),
                pltpu.VMEM((32, source_width), F32),
            ),
            in_specs=[far] * 6,
            out_specs=(vmem, vmem),
            scratch_shapes=[
                *(pltpu.VMEM(x.shape, x.dtype) for x in (sv, se, xv, xe, pb, ab)),
                pltpu.SemaphoreType.DMA((6,)),
                pltpu.VMEM((8, sv.shape[1]), F32),
                pltpu.VMEM((8, xv.shape[1]), F32),
                pltpu.VMEM((16, source_width), F32),
                pltpu.VMEM((64, slab_width), F32),
                pltpu.VMEM((slab_width, ROWS), BF16),
                pltpu.VMEM((slab_width, 128), F32),
                pltpu.VMEM((slab_width // 128, 32, 256), BF16),
                pltpu.VMEM((nw, ROWS, source_width), BF16),
                pltpu.VMEM((32, slab_width), F32),
                pltpu.VMEM((nw, 32, source_width), F32),
                pltpu.VMEM((nw, 32, source_width), F32),
                pltpu.VMEM((nl, 8, 128), F32),
                pltpu.VMEM((nl, 8, 128), F32),
                pltpu.SemaphoreType.DMA((nw,)),
                pltpu.SemaphoreType.DMA((nw,)),
                pltpu.SemaphoreType.DMA((nw,)),
                pltpu.SemaphoreType.DMA((nw,)),
                pltpu.SemaphoreType.DMA((nl,)),
                pltpu.SemaphoreType.DMA((nl,)),
                pltpu.SemaphoreType.REGULAR,
                pltpu.SemaphoreType.REGULAR,
                pltpu.SemaphoreType.REGULAR,
            ],
            compiler_params=pltpu.CompilerParams(collective_id=0, has_side_effects=True),
        )(sv, se, xv, xe, pb, ab)
        return pl.pallas_call(
            write_out,
            out_shape=(
                jax.ShapeDtypeStruct(primal.shape, F32),
                jax.ShapeDtypeStruct(adjoint.shape, F32),
            ),
            in_specs=[vmem, vmem],
            out_specs=(far, far),
            scratch_shapes=[pltpu.SemaphoreType.DMA((2,))],
        )(
            pltpu.with_memory_space_constraint(primal, pltpu.VMEM),
            pltpu.with_memory_space_constraint(adjoint, pltpu.VMEM),
        )

    return jax.shard_map(
        shards,
        mesh=mesh,
        in_specs=(
            P(None, "wide"),
            P(None, "wide"),
            P(None, ("wide", "long")),
            P(None, ("wide", "long")),
            P(None, ("wide", "long")),
            P(None, "wide"),
        ),
        out_specs=(P(None, ("wide", "long")), P(None, ("wide", "long"))),
        check_vma=False,
    )
```

```python
import functools
import math

import jax
import jax.numpy as jnp
from jax import lax
from jax.experimental import pallas as pl
from jax.experimental.pallas import tpu as pltpu
from jax.sharding import PartitionSpec as P

WAVENUMBER = 40.0
SOFTENING = 0.0004
AREA_WEIGHT = 0.05
TURNS = WAVENUMBER / (2.0 * math.pi)
SCALE = TURNS * TURNS
WEIGHT = TURNS / (4.0 * math.pi)
ROUND = 12582912.0
ROOT2 = math.sqrt(2.0)
SIN = tuple(ROOT2 * c for c in (3.14158202, -5.16714279, 2.54189895, -0.55463599))
COS = tuple(ROOT2 * c for c in (0.99999995, -4.93479286, 4.05841191, -1.33188013, 0.21969673))
ROWS = 48
GROUP = 3
EARLY = 3
PIECE = 32
MESH = pl.DeviceIdType.MESH
F32 = jnp.float32
BF16 = jnp.bfloat16


def split3(x):
    one = x.astype(BF16).astype(F32)
    rest = x - one
    two = rest.astype(BF16).astype(F32)
    three = (rest - two).astype(BF16).astype(F32)
    return one, two, three


def points(padded, ids, anchor):
    count, width = padded.shape[1], ids.shape[1]
    parts = jnp.concatenate(split3(padded), axis=0).astype(BF16)
    rows = lax.broadcasted_iota(jnp.int32, (count, width), 0) + anchor
    corners = []
    for corner in range(3):
        chosen = jnp.where(rows == ids[corner : corner + 1, :], 1.0, 0.0).astype(BF16)
        found = jnp.dot(parts, chosen, preferred_element_type=F32)
        corners.append(found[0:8] + found[8:16] + found[16:24])
    centre = (corners[0] + corners[1] + corners[2]) * (1.0 / 3.0) - 0.5
    one = corners[1] - corners[0]
    two = corners[2] - corners[0]
    ox, oy, oz = one[0:1], one[1:2], one[2:3]
    tx, ty, tz = two[0:1], two[1:2], two[2:3]
    nx = oy * tz - oz * ty
    ny = oz * tx - ox * tz
    nz = ox * ty - oy * tx
    area = 0.5 * jnp.sqrt(nx * nx + ny * ny + nz * nz)
    square = centre * centre
    norm = square[0:1] + square[1:2] + square[2:3]
    return centre, area, norm


def tile_values(scaled, weight):
    inverse = lax.rsqrt(scaled)
    turns = scaled * inverse
    part = turns - ((turns + ROUND) - ROUND)
    square = part * part
    sine = SIN[3]
    for c in SIN[2::-1]:
        sine = sine * square + c
    sine = sine * part
    cosine = COS[4]
    for c in COS[3::-1]:
        cosine = cosine * square + c
    heavy = weight * inverse
    bent = heavy * sine
    return (heavy - bent * sine).astype(BF16), (bent * cosine).astype(BF16)


def kernel(
    nw, nl, sv_far, se_far, xv_far, xe_far, pb_far, ab_far, primal_out, adjoint_out,
    sv, se, xv, xe, pb, ab, arrived,
    slab_pad, source_pad, source_rows, slab_rows, features, areas, adjoint_pack,
    gathered, primal_acc, adjoint_send, adjoint_recv, primal_send, primal_recv,
    gather_out, gather_in, adjoint_go, adjoint_in, primal_go, primal_in, known_y, known_z, known_all,
):
    wide_at = lax.axis_index("wide")
    long_at = lax.axis_index("long")
    slab_width = se.shape[1]
    source_width = xe.shape[1]
    blocks = slab_width // 128

    barrier = pltpu.get_barrier_semaphore()

    def greet_wide(k, carry):
        pl.semaphore_signal(
            barrier, inc=1, device_id=(lax.rem(wide_at + k, nw), long_at), device_id_type=MESH
        )
        return carry

    def beside(step, size, by):
        place = (long_at // step) % size
        return long_at + ((place + by) % size - place) * step

    def greet_ring(semaphore, step):
        for by in (1, 3):
            pl.semaphore_signal(
                semaphore, inc=1, device_id=(wide_at, beside(step, 4, by)), device_id_type=MESH
            )

    lax.fori_loop(1, nw, greet_wide, 0)
    greet_ring(barrier, 4)
    greet_ring(barrier, 1)

    fetches = [
        pltpu.make_async_copy(far, near, arrived.at[n])
        for n, (far, near) in enumerate(
            ((xv_far, xv), (xe_far, xe), (pb_far, pb), (sv_far, sv), (se_far, se), (ab_far, ab))
        )
    ]
    for fetch in fetches:
        fetch.start()

    for fetch in fetches[:3]:
        fetch.wait()
    source_pad[...] = jnp.zeros_like(source_pad)
    source_pad[0:3, :] = xv[...]
    anchor = (wide_at * nl + long_at) * (source_width // 2)
    centre, area, norm = points(source_pad[...], xe[...], anchor)
    for n, piece in enumerate(split3(centre * (-2.0 * SCALE))):
        source_rows[3 * n : 3 * n + 3, :] = piece[0:3]
    for n, piece in enumerate(split3(SCALE * (norm + AREA_WEIGHT * area))):
        source_rows[9 + n : 10 + n, :] = piece
    source_rows[12:13, :] = jnp.ones((1, source_width), F32)
    for n, piece in enumerate(split3(area)):
        source_rows[13 + n : 14 + n, :] = piece
    gathered[0, 0:32, :] = pb[...]
    gathered[0, 32:48, :] = source_rows[...].astype(BF16)

    pl.semaphore_wait(barrier, nw - 1 + 4)

    def gather_copy(k):
        return pltpu.make_async_remote_copy(
            src_ref=gathered.at[0],
            dst_ref=gathered.at[k],
            send_sem=gather_out.at[k],
            recv_sem=gather_in.at[k],
            device_id=(lax.rem(wide_at + nw - k, nw), long_at),
            device_id_type=MESH,
        )

    def gather_start(k, carry):
        gather_copy(k).start()
        return carry

    lax.fori_loop(1, nw, gather_start, 0)
    greet_ring(known_y, 4)

    for fetch in fetches[3:]:
        fetch.wait()
    slab_pad[...] = jnp.zeros_like(slab_pad)
    slab_pad[0:3, :] = sv[...]
    centre, area, norm = points(slab_pad[...], se[...], wide_at * (slab_width // 2))
    one, two, three = (piece[0:3] for piece in split3(centre))
    norms = split3(SCALE * (norm + SOFTENING + AREA_WEIGHT * area))
    slab_rows[...] = jnp.zeros_like(slab_rows)
    for n in range(3):
        slab_rows[3 * n : 3 * n + 3, :] = one
        slab_rows[9 + n : 10 + n, :] = jnp.ones((1, slab_width), F32)
        slab_rows[16 * n + 12 : 16 * n + 13, :] = norms[n]
    for n in range(2):
        slab_rows[16 + 3 * n : 19 + 3 * n, :] = two
    slab_rows[32:35, :] = three
    slab_rows[48:49, :] = WEIGHT * area
    turned = slab_rows[...].T
    features[...] = turned[:, 0:ROWS].astype(BF16)
    areas[...] = jnp.broadcast_to(turned[:, 48:49], areas.shape)

    rows = ab[...]
    crossed = jnp.concatenate([rows[16:32], -rows[0:16]], axis=0)
    for b in range(blocks):
        adjoint_pack[b, :, 0:128] = rows[:, 128 * b : 128 * b + 128]
        adjoint_pack[b, :, 128:256] = crossed[:, 128 * b : 128 * b + 128]
    primal_acc[...] = jnp.zeros_like(primal_acc)

    def adjoint_copy(k):
        return pltpu.make_async_remote_copy(
            src_ref=adjoint_send.at[k],
            dst_ref=adjoint_recv.at[k],
            send_sem=adjoint_go.at[k],
            recv_sem=adjoint_in.at[k],
            device_id=(lax.rem(wide_at + k, nw), long_at),
            device_id_type=MESH,
        )

    def at_block(b, start=0, size=128):
        if isinstance(b, int):
            return pl.ds(128 * b + start, size)
        return pl.ds(pl.multiple_of(128 * b + start, size), size)

    def distances(k, b):
        source = gathered[k, 32:48, :]
        stacked = jnp.concatenate([source, source, source], axis=0)
        return jnp.dot(features[at_block(b), :], stacked, preferred_element_type=F32)

    def values(k, b, distance):
        source = gathered[k, 32:48, :].astype(F32)
        source_area = source[13:14] + source[14:15] + source[15:16]
        reals, imags = [], []
        for q in range(128 // PIECE):
            weight = areas[at_block(b, PIECE * q, PIECE), :] * source_area
            real, imag = tile_values(distance[PIECE * q : PIECE * q + PIECE, :], weight)
            reals.append(real)
            imags.append(imag)
        return jnp.concatenate(reals, axis=0), jnp.concatenate(imags, axis=0)

    def images(k, b, real, imag):
        columns = gathered[k, 0:32, :]
        turned_columns = jnp.concatenate([-columns[16:32], columns[0:16]], axis=0)
        primal_acc[:, at_block(b)] += lax.dot_general(
            jnp.concatenate([columns, turned_columns], axis=1),
            jnp.concatenate([real, imag], axis=1),
            (((1,), (1,)), ((), ())),
            preferred_element_type=F32,
        )
        return jnp.dot(
            adjoint_pack[b], jnp.concatenate([real, imag], axis=0), preferred_element_type=F32
        )

    def process(todo, chunks):
        totals = {}
        ahead = distances(*todo[0])
        behind = None

        def finish(k, b, pair):
            term = images(k, b, *pair)
            name = chunks[id(k)]
            totals[name] = term if name not in totals else totals[name] + term

        for n, (k, b) in enumerate(todo):
            distance = ahead
            if n + 1 < len(todo):
                ahead = distances(*todo[n + 1])
            if behind is not None:
                finish(*behind)
            behind = (k, b, values(k, b, distance))
        finish(*behind)
        return totals

    def by_chunk(slots):
        chunks = {id(k): n for n, k in enumerate(slots)}
        totals = process([(k, b) for k in slots for b in range(blocks)], chunks)
        for n, k in enumerate(slots):
            adjoint_send[k] = totals[n]

    def step(g, carry):
        first = 1 + g * GROUP
        for c in range(GROUP):
            gather_copy(first + c).wait_recv()
        by_chunk([first + c for c in range(GROUP)])
        for c in range(GROUP):
            adjoint_copy(first + c).start()

        @pl.when(g == 0)
        def _():
            pl.semaphore_wait(known_z, 2)
            greet_ring(known_all, 1)

        return carry

    by_chunk([0])
    pl.semaphore_wait(known_y, 2)
    greet_ring(known_z, 1)
    lax.fori_loop(0, EARLY, step, 0)

    rest = list(range(1 + EARLY * GROUP, nw))
    for k in rest:
        gather_copy(k).wait_recv()
        adjoint_send[k] = jnp.zeros((32, 128), F32)
    lane = lax.broadcasted_iota(jnp.int32, (8, 128), 1) // 32

    def primal_copy(k):
        peer = lax.rem(long_at + k, nl)
        return pltpu.make_async_remote_copy(
            src_ref=primal_send.at[peer],
            dst_ref=primal_recv.at[k],
            send_sem=primal_go.at[k],
            recv_sem=primal_in.at[k],
            device_id=(wide_at, peer),
            device_id_type=MESH,
        )

    def block_step(b, carry):
        totals = process([(k, b) for k in rest], {id(k): k for k in rest})
        for k in rest:
            adjoint_send[k] += totals[k]

        held = [primal_acc[8 * j : 8 * j + 8, at_block(b)] for j in range(4)]
        for q in range(4):
            piece = jnp.zeros((8, 128), F32)
            for j in range(4):
                shift = (32 * (j - q)) % 128
                moved = held[j] if shift == 0 else pltpu.roll(held[j], shift, 1)
                piece = jnp.where(lane == j, moved, piece)
            primal_send[4 * b + q] = piece

        @pl.when(b == 0)
        def _():
            pl.semaphore_wait(known_all, 2)

        for q in range(4):
            ahead = lax.rem(4 * b + q + nl - long_at, nl)

            @pl.when(ahead > 0)
            def _():
                primal_copy(ahead).start()

        return carry

    lax.fori_loop(0, blocks, block_step, 0)
    for k in rest:
        adjoint_copy(k).start()

    def adjoint_sum(k, total):
        adjoint_copy(k).wait_recv()
        return total + adjoint_recv[k]

    adjoint_out[...] = lax.fori_loop(1, nw, adjoint_sum, adjoint_send[0])

    def primal_sum(k, total):
        primal_copy(k).wait_recv()
        return total + primal_recv[k]

    total = lax.fori_loop(1, nl, primal_sum, primal_send[long_at])
    for j in range(4):
        primal_out[8 * j : 8 * j + 8, :] = total[:, 32 * j : 32 * j + 32]

    def finish_wide(k, carry):
        gather_copy(k).wait_send()
        adjoint_copy(k).wait_send()
        return carry

    def finish_long(k, carry):
        primal_copy(k).wait_send()
        return carry

    lax.fori_loop(1, nw, finish_wide, 0)
    lax.fori_loop(1, nl, finish_long, 0)


def write_out(primal, adjoint, primal_out, adjoint_out, done):
    one = pltpu.make_async_copy(primal, primal_out, done.at[0])
    two = pltpu.make_async_copy(adjoint, adjoint_out, done.at[1])
    one.start()
    two.start()
    one.wait()
    two.wait()


def solution(mesh):
    nw, nl = mesh.shape["wide"], mesh.shape["long"]

    def shards(sv, se, xv, xe, pb, ab):
        slab_width, source_width = se.shape[1], xe.shape[1]
        far = pl.BlockSpec(memory_space=pl.ANY)
        vmem = pl.BlockSpec(memory_space=pltpu.VMEM)
        primal, adjoint = pl.pallas_call(
            functools.partial(kernel, nw, nl),
            out_shape=(
                pltpu.VMEM((32, slab_width // nl), F32),
                pltpu.VMEM((32, source_width), F32),
            ),
            in_specs=[far] * 6,
            out_specs=(vmem, vmem),
            scratch_shapes=[
                *(pltpu.VMEM(x.shape, x.dtype) for x in (sv, se, xv, xe, pb, ab)),
                pltpu.SemaphoreType.DMA((6,)),
                pltpu.VMEM((8, sv.shape[1]), F32),
                pltpu.VMEM((8, xv.shape[1]), F32),
                pltpu.VMEM((16, source_width), F32),
                pltpu.VMEM((64, slab_width), F32),
                pltpu.VMEM((slab_width, ROWS), BF16),
                pltpu.VMEM((slab_width, 128), F32),
                pltpu.VMEM((slab_width // 128, 32, 256), BF16),
                pltpu.VMEM((nw, ROWS, source_width), BF16),
                pltpu.VMEM((32, slab_width), F32),
                pltpu.VMEM((nw, 32, source_width), F32),
                pltpu.VMEM((nw, 32, source_width), F32),
                pltpu.VMEM((nl, 8, 128), F32),
                pltpu.VMEM((nl, 8, 128), F32),
                pltpu.SemaphoreType.DMA((nw,)),
                pltpu.SemaphoreType.DMA((nw,)),
                pltpu.SemaphoreType.DMA((nw,)),
                pltpu.SemaphoreType.DMA((nw,)),
                pltpu.SemaphoreType.DMA((nl,)),
                pltpu.SemaphoreType.DMA((nl,)),
                pltpu.SemaphoreType.REGULAR,
                pltpu.SemaphoreType.REGULAR,
                pltpu.SemaphoreType.REGULAR,
            ],
            compiler_params=pltpu.CompilerParams(collective_id=0, has_side_effects=True),
        )(sv, se, xv, xe, pb, ab)
        return pl.pallas_call(
            write_out,
            out_shape=(
                jax.ShapeDtypeStruct(primal.shape, F32),
                jax.ShapeDtypeStruct(adjoint.shape, F32),
            ),
            in_specs=[vmem, vmem],
            out_specs=(far, far),
            scratch_shapes=[pltpu.SemaphoreType.DMA((2,))],
        )(
            pltpu.with_memory_space_constraint(primal, pltpu.VMEM),
            pltpu.with_memory_space_constraint(adjoint, pltpu.VMEM),
        )

    return jax.shard_map(
        shards,
        mesh=mesh,
        in_specs=(
            P(None, "wide"),
            P(None, "wide"),
            P(None, ("wide", "long")),
            P(None, ("wide", "long")),
            P(None, ("wide", "long")),
            P(None, "wide"),
        ),
        out_specs=(P(None, ("wide", "long")), P(None, ("wide", "long"))),
        check_vma=False,
    )
```

```python
import functools
import math

import jax
import jax.numpy as jnp
from jax import lax
from jax.experimental import pallas as pl
from jax.experimental.pallas import tpu as pltpu
from jax.sharding import PartitionSpec as P

WAVENUMBER = 40.0
SOFTENING = 0.0004
AREA_WEIGHT = 0.05
TURNS = WAVENUMBER / (2.0 * math.pi)
SCALE = TURNS * TURNS
WEIGHT = TURNS / (4.0 * math.pi)
ROUND = 12582912.0
ROOT2 = math.sqrt(2.0)
SIN = tuple(ROOT2 * c for c in (3.14158202, -5.16714279, 2.54189895, -0.55463599))
COS = tuple(ROOT2 * c for c in (0.99999995, -4.93479286, 4.05841191, -1.33188013, 0.21969673))
ROWS = 48


PIECE = 32
MESH = pl.DeviceIdType.MESH
F32 = jnp.float32
BF16 = jnp.bfloat16


def split3(x):
    one = x.astype(BF16).astype(F32)
    rest = x - one
    two = rest.astype(BF16).astype(F32)
    three = (rest - two).astype(BF16).astype(F32)
    return one, two, three


def points(padded, ids, anchor):
    count, width = padded.shape[1], ids.shape[1]
    parts = jnp.concatenate(split3(padded), axis=0).astype(BF16)
    rows = lax.broadcasted_iota(jnp.int32, (count, width), 0) + anchor
    corners = []
    for corner in range(3):
        chosen = jnp.where(rows == ids[corner : corner + 1, :], 1.0, 0.0).astype(BF16)
        found = jnp.dot(parts, chosen, preferred_element_type=F32)
        corners.append(found[0:8] + found[8:16] + found[16:24])
    centre = (corners[0] + corners[1] + corners[2]) * (1.0 / 3.0) - 0.5
    one = corners[1] - corners[0]
    two = corners[2] - corners[0]
    ox, oy, oz = one[0:1], one[1:2], one[2:3]
    tx, ty, tz = two[0:1], two[1:2], two[2:3]
    nx = oy * tz - oz * ty
    ny = oz * tx - ox * tz
    nz = ox * ty - oy * tx
    area = 0.5 * jnp.sqrt(nx * nx + ny * ny + nz * nz)
    square = centre * centre
    norm = square[0:1] + square[1:2] + square[2:3]
    return centre, area, norm


def tile_values(scaled, weight):
    inverse = lax.rsqrt(scaled)
    turns = scaled * inverse
    part = turns - ((turns + ROUND) - ROUND)
    square = part * part
    sine = SIN[3]
    for c in SIN[2::-1]:
        sine = sine * square + c
    sine = sine * part
    cosine = COS[4]
    for c in COS[3::-1]:
        cosine = cosine * square + c
    heavy = weight * inverse
    bent = heavy * sine
    return (heavy - bent * sine).astype(BF16), (bent * cosine).astype(BF16)


def kernel(
    nw, nl, sv_far, se_far, xv_far, xe_far, pb_far, ab_far, primal_out, adjoint_out,
    sv, se, xv, xe, pb, ab, arrived,
    slab_pad, source_pad, source_rows, slab_rows, features, areas, adjoint_pack,
    gathered, primal_acc, adjoint_send, adjoint_recv, primal_send, primal_recv,
    gather_out, gather_in, adjoint_go, adjoint_in, primal_go, primal_in, known_y, known_z, known_all,
):
    wide_at = lax.axis_index("wide")
    long_at = lax.axis_index("long")
    slab_width = se.shape[1]
    source_width = xe.shape[1]
    blocks = slab_width // 128

    barrier = pltpu.get_barrier_semaphore()

    def greet_wide(k, carry):
        pl.semaphore_signal(
            barrier, inc=1, device_id=(lax.rem(wide_at + k, nw), long_at), device_id_type=MESH
        )
        return carry

    def beside(step, size, by):
        place = (long_at // step) % size
        return long_at + ((place + by) % size - place) * step

    def greet_ring(semaphore, step):
        for by in (1, 3):
            pl.semaphore_signal(
                semaphore, inc=1, device_id=(wide_at, beside(step, 4, by)), device_id_type=MESH
            )

    lax.fori_loop(1, nw, greet_wide, 0)
    greet_ring(barrier, 4)
    greet_ring(barrier, 1)

    fetches = [
        pltpu.make_async_copy(far, near, arrived.at[n])
        for n, (far, near) in enumerate(
            ((xv_far, xv), (xe_far, xe), (pb_far, pb), (sv_far, sv), (se_far, se), (ab_far, ab))
        )
    ]
    for fetch in fetches:
        fetch.start()

    for fetch in fetches[:3]:
        fetch.wait()
    source_pad[...] = jnp.zeros_like(source_pad)
    source_pad[0:3, :] = xv[...]
    anchor = (wide_at * nl + long_at) * (source_width // 2)
    centre, area, norm = points(source_pad[...], xe[...], anchor)
    for n, piece in enumerate(split3(centre * (-2.0 * SCALE))):
        source_rows[3 * n : 3 * n + 3, :] = piece[0:3]
    for n, piece in enumerate(split3(SCALE * (norm + AREA_WEIGHT * area))):
        source_rows[9 + n : 10 + n, :] = piece
    source_rows[12:13, :] = jnp.ones((1, source_width), F32)
    for n, piece in enumerate(split3(area)):
        source_rows[13 + n : 14 + n, :] = piece
    gathered[0, 0:32, :] = pb[...]
    gathered[0, 32:48, :] = source_rows[...].astype(BF16)

    pl.semaphore_wait(barrier, nw - 1 + 4)

    def gather_copy(k):
        return pltpu.make_async_remote_copy(
            src_ref=gathered.at[0],
            dst_ref=gathered.at[k],
            send_sem=gather_out.at[k],
            recv_sem=gather_in.at[k],
            device_id=(lax.rem(wide_at + nw - k, nw), long_at),
            device_id_type=MESH,
        )

    def gather_start(k, carry):
        gather_copy(k).start()
        return carry

    lax.fori_loop(1, nw, gather_start, 0)
    greet_ring(known_y, 4)

    for fetch in fetches[3:]:
        fetch.wait()
    slab_pad[...] = jnp.zeros_like(slab_pad)
    slab_pad[0:3, :] = sv[...]
    centre, area, norm = points(slab_pad[...], se[...], wide_at * (slab_width // 2))
    one, two, three = (piece[0:3] for piece in split3(centre))
    norms = split3(SCALE * (norm + SOFTENING + AREA_WEIGHT * area))
    slab_rows[...] = jnp.zeros_like(slab_rows)
    for n in range(3):
        slab_rows[3 * n : 3 * n + 3, :] = one
        slab_rows[9 + n : 10 + n, :] = jnp.ones((1, slab_width), F32)
        slab_rows[16 * n + 12 : 16 * n + 13, :] = norms[n]
    for n in range(2):
        slab_rows[16 + 3 * n : 19 + 3 * n, :] = two
    slab_rows[32:35, :] = three
    slab_rows[48:49, :] = WEIGHT * area
    turned = slab_rows[...].T
    features[...] = turned[:, 0:ROWS].astype(BF16)
    areas[...] = jnp.broadcast_to(turned[:, 48:49], areas.shape)

    rows = ab[...]
    crossed = jnp.concatenate([rows[16:32], -rows[0:16]], axis=0)
    for b in range(blocks):
        adjoint_pack[b, :, 0:128] = rows[:, 128 * b : 128 * b + 128]
        adjoint_pack[b, :, 128:256] = crossed[:, 128 * b : 128 * b + 128]
    primal_acc[...] = jnp.zeros_like(primal_acc)

    def adjoint_copy(k):
        return pltpu.make_async_remote_copy(
            src_ref=adjoint_send.at[k],
            dst_ref=adjoint_recv.at[k],
            send_sem=adjoint_go.at[k],
            recv_sem=adjoint_in.at[k],
            device_id=(lax.rem(wide_at + k, nw), long_at),
            device_id_type=MESH,
        )

    def at_block(b, start=0, size=128):
        if isinstance(b, int):
            return pl.ds(128 * b + start, size)
        return pl.ds(pl.multiple_of(128 * b + start, size), size)

    def distances(k, b):
        source = gathered[k, 32:48, :]
        stacked = jnp.concatenate([source, source, source], axis=0)
        return jnp.dot(features[at_block(b), :], stacked, preferred_element_type=F32)

    def values(k, b, distance):
        source = gathered[k, 32:48, :].astype(F32)
        source_area = source[13:14] + source[14:15] + source[15:16]
        reals, imags = [], []
        for q in range(128 // PIECE):
            weight = areas[at_block(b, PIECE * q, PIECE), :] * source_area
            real, imag = tile_values(distance[PIECE * q : PIECE * q + PIECE, :], weight)
            reals.append(real)
            imags.append(imag)
        return jnp.concatenate(reals, axis=0), jnp.concatenate(imags, axis=0)

    def images(k, b, real, imag):
        columns = gathered[k, 0:32, :]
        turned_columns = jnp.concatenate([-columns[16:32], columns[0:16]], axis=0)
        primal_acc[:, at_block(b)] += lax.dot_general(
            jnp.concatenate([columns, turned_columns], axis=1),
            jnp.concatenate([real, imag], axis=1),
            (((1,), (1,)), ((), ())),
            preferred_element_type=F32,
        )
        return jnp.dot(
            adjoint_pack[b], jnp.concatenate([real, imag], axis=0), preferred_element_type=F32
        )

    def process(todo, chunks):
        totals = {}
        ahead = distances(*todo[0])
        behind = None

        def finish(k, b, pair):
            term = images(k, b, *pair)
            name = chunks[id(k)]
            totals[name] = term if name not in totals else totals[name] + term

        for n, (k, b) in enumerate(todo):
            distance = ahead
            if n + 1 < len(todo):
                ahead = distances(*todo[n + 1])
            if behind is not None:
                finish(*behind)
            behind = (k, b, values(k, b, distance))
        finish(*behind)
        return totals

    def by_chunk(slots):
        chunks = {id(k): n for n, k in enumerate(slots)}
        totals = process([(k, b) for k in slots for b in range(blocks)], chunks)
        for n, k in enumerate(slots):
            adjoint_send[k] = totals[n]

    def early(slots):
        for k in slots:
            gather_copy(k).wait_recv()
        by_chunk(slots)
        for k in slots:
            adjoint_copy(k).start()

    by_chunk([0])
    pl.semaphore_wait(known_y, 2)
    greet_ring(known_z, 1)
    early([1, 2, 3])
    pl.semaphore_wait(known_z, 2)
    greet_ring(known_all, 1)
    early([4, 5, 6, 7, 8])

    rest = list(range(9, nw))
    for k in rest:
        gather_copy(k).wait_recv()
        adjoint_send[k] = jnp.zeros((32, 128), F32)
    lane = lax.broadcasted_iota(jnp.int32, (8, 128), 1) // 32

    def primal_copy(k):
        peer = lax.rem(long_at + k, nl)
        return pltpu.make_async_remote_copy(
            src_ref=primal_send.at[peer],
            dst_ref=primal_recv.at[k],
            send_sem=primal_go.at[k],
            recv_sem=primal_in.at[k],
            device_id=(wide_at, peer),
            device_id_type=MESH,
        )

    def block_step(b, carry):
        totals = process([(k, b) for k in rest], {id(k): k for k in rest})
        for k in rest:
            adjoint_send[k] += totals[k]

        held = [primal_acc[8 * j : 8 * j + 8, at_block(b)] for j in range(4)]
        for q in range(4):
            piece = jnp.zeros((8, 128), F32)
            for j in range(4):
                shift = (32 * (j - q)) % 128
                moved = held[j] if shift == 0 else pltpu.roll(held[j], shift, 1)
                piece = jnp.where(lane == j, moved, piece)
            primal_send[4 * b + q] = piece

        @pl.when(b == 0)
        def _():
            pl.semaphore_wait(known_all, 2)

        for q in range(4):
            ahead = lax.rem(4 * b + q + nl - long_at, nl)

            @pl.when(ahead > 0)
            def _():
                primal_copy(ahead).start()

        return carry

    lax.fori_loop(0, blocks, block_step, 0)
    for k in rest:
        adjoint_copy(k).start()

    total = adjoint_send[0]
    for k in range(1, nw):
        adjoint_copy(k).wait_recv()
        total = total + adjoint_recv[k]
    adjoint_out[...] = total

    def finish_wide(k, carry):
        gather_copy(k).wait_send()
        adjoint_copy(k).wait_send()
        return carry

    def finish_long(k, carry):
        primal_copy(k).wait_send()
        return carry

    lax.fori_loop(1, nw, finish_wide, 0)
    lax.fori_loop(1, nl, finish_long, 0)

    total = primal_send[long_at]
    for k in range(1, nl):
        primal_copy(k).wait_recv()
        total = total + primal_recv[k]
    for j in range(4):
        primal_out[8 * j : 8 * j + 8, :] = total[:, 32 * j : 32 * j + 32]


def write_out(primal, adjoint, primal_out, adjoint_out, done):
    one = pltpu.make_async_copy(primal, primal_out, done.at[0])
    two = pltpu.make_async_copy(adjoint, adjoint_out, done.at[1])
    one.start()
    two.start()
    one.wait()
    two.wait()


def solution(mesh):
    nw, nl = mesh.shape["wide"], mesh.shape["long"]

    def shards(sv, se, xv, xe, pb, ab):
        slab_width, source_width = se.shape[1], xe.shape[1]
        far = pl.BlockSpec(memory_space=pl.ANY)
        vmem = pl.BlockSpec(memory_space=pltpu.VMEM)
        primal, adjoint = pl.pallas_call(
            functools.partial(kernel, nw, nl),
            out_shape=(
                pltpu.VMEM((32, slab_width // nl), F32),
                pltpu.VMEM((32, source_width), F32),
            ),
            in_specs=[far] * 6,
            out_specs=(vmem, vmem),
            scratch_shapes=[
                *(pltpu.VMEM(x.shape, x.dtype) for x in (sv, se, xv, xe, pb, ab)),
                pltpu.SemaphoreType.DMA((6,)),
                pltpu.VMEM((8, sv.shape[1]), F32),
                pltpu.VMEM((8, xv.shape[1]), F32),
                pltpu.VMEM((16, source_width), F32),
                pltpu.VMEM((64, slab_width), F32),
                pltpu.VMEM((slab_width, ROWS), BF16),
                pltpu.VMEM((slab_width, 128), F32),
                pltpu.VMEM((slab_width // 128, 32, 256), BF16),
                pltpu.VMEM((nw, ROWS, source_width), BF16),
                pltpu.VMEM((32, slab_width), F32),
                pltpu.VMEM((nw, 32, source_width), F32),
                pltpu.VMEM((nw, 32, source_width), F32),
                pltpu.VMEM((nl, 8, 128), F32),
                pltpu.VMEM((nl, 8, 128), F32),
                pltpu.SemaphoreType.DMA((nw,)),
                pltpu.SemaphoreType.DMA((nw,)),
                pltpu.SemaphoreType.DMA((nw,)),
                pltpu.SemaphoreType.DMA((nw,)),
                pltpu.SemaphoreType.DMA((nl,)),
                pltpu.SemaphoreType.DMA((nl,)),
                pltpu.SemaphoreType.REGULAR,
                pltpu.SemaphoreType.REGULAR,
                pltpu.SemaphoreType.REGULAR,
            ],
            compiler_params=pltpu.CompilerParams(collective_id=0, has_side_effects=True),
        )(sv, se, xv, xe, pb, ab)
        return pl.pallas_call(
            write_out,
            out_shape=(
                jax.ShapeDtypeStruct(primal.shape, F32),
                jax.ShapeDtypeStruct(adjoint.shape, F32),
            ),
            in_specs=[vmem, vmem],
            out_specs=(far, far),
            scratch_shapes=[pltpu.SemaphoreType.DMA((2,))],
        )(
            pltpu.with_memory_space_constraint(primal, pltpu.VMEM),
            pltpu.with_memory_space_constraint(adjoint, pltpu.VMEM),
        )

    return jax.shard_map(
        shards,
        mesh=mesh,
        in_specs=(
            P(None, "wide"),
            P(None, "wide"),
            P(None, ("wide", "long")),
            P(None, ("wide", "long")),
            P(None, ("wide", "long")),
            P(None, "wide"),
        ),
        out_specs=(P(None, ("wide", "long")), P(None, ("wide", "long"))),
        check_vma=False,
    )
```

```python
import functools
import math

import jax
import jax.numpy as jnp
from jax import lax
from jax.experimental import pallas as pl
from jax.experimental.pallas import tpu as pltpu
from jax.sharding import PartitionSpec as P

WAVENUMBER = 40.0
SOFTENING = 0.0004
AREA_WEIGHT = 0.05
TURNS = WAVENUMBER / (2.0 * math.pi)
SCALE = TURNS * TURNS
WEIGHT = TURNS / (4.0 * math.pi)
ROUND = 12582912.0
ROOT2 = math.sqrt(2.0)
SIN = tuple(ROOT2 * c for c in (3.14158202, -5.16714279, 2.54189895, -0.55463599))
COS = tuple(ROOT2 * c for c in (0.99999995, -4.93479286, 4.05841191, -1.33188013, 0.21969673))
ROWS = 48


PIECE = 32
MESH = pl.DeviceIdType.MESH
F32 = jnp.float32
BF16 = jnp.bfloat16


def split3(x):
    one = x.astype(BF16).astype(F32)
    rest = x - one
    two = rest.astype(BF16).astype(F32)
    three = (rest - two).astype(BF16).astype(F32)
    return one, two, three


def points(padded, ids, anchor):
    count, width = padded.shape[1], ids.shape[1]
    parts = jnp.concatenate(split3(padded), axis=0).astype(BF16)
    rows = lax.broadcasted_iota(jnp.int32, (count, width), 0) + anchor
    corners = []
    for corner in range(3):
        chosen = jnp.where(rows == ids[corner : corner + 1, :], 1.0, 0.0).astype(BF16)
        found = jnp.dot(parts, chosen, preferred_element_type=F32)
        corners.append(found[0:8] + found[8:16] + found[16:24])
    centre = (corners[0] + corners[1] + corners[2]) * (1.0 / 3.0) - 0.5
    one = corners[1] - corners[0]
    two = corners[2] - corners[0]
    ox, oy, oz = one[0:1], one[1:2], one[2:3]
    tx, ty, tz = two[0:1], two[1:2], two[2:3]
    nx = oy * tz - oz * ty
    ny = oz * tx - ox * tz
    nz = ox * ty - oy * tx
    area = 0.5 * jnp.sqrt(nx * nx + ny * ny + nz * nz)
    square = centre * centre
    norm = square[0:1] + square[1:2] + square[2:3]
    return centre, area, norm


def tile_values(scaled, weight):
    inverse = lax.rsqrt(scaled)
    turns = scaled * inverse
    part = turns - ((turns + ROUND) - ROUND)
    square = part * part
    sine = SIN[3]
    for c in SIN[2::-1]:
        sine = sine * square + c
    sine = sine * part
    cosine = COS[4]
    for c in COS[3::-1]:
        cosine = cosine * square + c
    heavy = weight * inverse
    bent = heavy * sine
    return (heavy - bent * sine).astype(BF16), (bent * cosine).astype(BF16)


def kernel(
    nw, nl, sv_far, se_far, xv_far, xe_far, pb_far, ab_far, primal_out, adjoint_out,
    sv, se, xv, xe, pb, ab, arrived,
    slab_pad, source_pad, source_rows, slab_rows, features, areas, adjoint_pack,
    gathered, primal_acc, adjoint_send, adjoint_recv, primal_send, primal_recv,
    gather_out, gather_in, adjoint_go, adjoint_in, primal_go, primal_in, known_y, known_z, known_all,
):
    wide_at = lax.axis_index("wide")
    long_at = lax.axis_index("long")
    slab_width = se.shape[1]
    source_width = xe.shape[1]
    blocks = slab_width // 128

    barrier = pltpu.get_barrier_semaphore()

    def greet_wide(k, carry):
        pl.semaphore_signal(
            barrier, inc=1, device_id=(lax.rem(wide_at + k, nw), long_at), device_id_type=MESH
        )
        return carry

    def beside(step, size, by):
        place = (long_at // step) % size
        return long_at + ((place + by) % size - place) * step

    def greet_ring(semaphore, step):
        for by in (1, 3):
            pl.semaphore_signal(
                semaphore, inc=1, device_id=(wide_at, beside(step, 4, by)), device_id_type=MESH
            )

    lax.fori_loop(1, nw, greet_wide, 0)
    greet_ring(barrier, 4)
    greet_ring(barrier, 1)

    fetches = [
        pltpu.make_async_copy(far, near, arrived.at[n])
        for n, (far, near) in enumerate(
            ((xv_far, xv), (xe_far, xe), (pb_far, pb), (sv_far, sv), (se_far, se), (ab_far, ab))
        )
    ]
    for fetch in fetches:
        fetch.start()

    for fetch in fetches[:3]:
        fetch.wait()
    source_pad[...] = jnp.zeros_like(source_pad)
    source_pad[0:3, :] = xv[...]
    anchor = (wide_at * nl + long_at) * (source_width // 2)
    centre, area, norm = points(source_pad[...], xe[...], anchor)
    for n, piece in enumerate(split3(centre * (-2.0 * SCALE))):
        source_rows[3 * n : 3 * n + 3, :] = piece[0:3]
    for n, piece in enumerate(split3(SCALE * (norm + AREA_WEIGHT * area))):
        source_rows[9 + n : 10 + n, :] = piece
    source_rows[12:13, :] = jnp.ones((1, source_width), F32)
    for n, piece in enumerate(split3(area)):
        source_rows[13 + n : 14 + n, :] = piece
    gathered[0, 0:32, :] = pb[...]
    gathered[0, 32:48, :] = source_rows[...].astype(BF16)

    pl.semaphore_wait(barrier, nw - 1 + 4)

    def gather_copy(k):
        return pltpu.make_async_remote_copy(
            src_ref=gathered.at[0],
            dst_ref=gathered.at[k],
            send_sem=gather_out.at[k],
            recv_sem=gather_in.at[k],
            device_id=(lax.rem(wide_at + nw - k, nw), long_at),
            device_id_type=MESH,
        )

    def gather_start(k, carry):
        gather_copy(k).start()
        return carry

    lax.fori_loop(1, nw, gather_start, 0)
    greet_ring(known_y, 4)

    for fetch in fetches[3:]:
        fetch.wait()
    slab_pad[...] = jnp.zeros_like(slab_pad)
    slab_pad[0:3, :] = sv[...]
    centre, area, norm = points(slab_pad[...], se[...], wide_at * (slab_width // 2))
    one, two, three = (piece[0:3] for piece in split3(centre))
    norms = split3(SCALE * (norm + SOFTENING + AREA_WEIGHT * area))
    slab_rows[...] = jnp.zeros_like(slab_rows)
    for n in range(3):
        slab_rows[3 * n : 3 * n + 3, :] = one
        slab_rows[9 + n : 10 + n, :] = jnp.ones((1, slab_width), F32)
        slab_rows[16 * n + 12 : 16 * n + 13, :] = norms[n]
    for n in range(2):
        slab_rows[16 + 3 * n : 19 + 3 * n, :] = two
    slab_rows[32:35, :] = three
    slab_rows[48:49, :] = WEIGHT * area
    turned = slab_rows[...].T
    features[...] = turned[:, 0:ROWS].astype(BF16)
    areas[...] = jnp.broadcast_to(turned[:, 48:49], areas.shape)

    rows = ab[...]
    crossed = jnp.concatenate([rows[16:32], -rows[0:16]], axis=0)
    for b in range(blocks):
        adjoint_pack[b, :, 0:128] = rows[:, 128 * b : 128 * b + 128]
        adjoint_pack[b, :, 128:256] = crossed[:, 128 * b : 128 * b + 128]
    primal_acc[...] = jnp.zeros_like(primal_acc)

    def adjoint_copy(k):
        return pltpu.make_async_remote_copy(
            src_ref=adjoint_send.at[k],
            dst_ref=adjoint_recv.at[k],
            send_sem=adjoint_go.at[k],
            recv_sem=adjoint_in.at[k],
            device_id=(lax.rem(wide_at + k, nw), long_at),
            device_id_type=MESH,
        )

    def at_block(b, start=0, size=128):
        if isinstance(b, int):
            return pl.ds(128 * b + start, size)
        return pl.ds(pl.multiple_of(128 * b + start, size), size)

    def distances(k, b):
        source = gathered[k, 32:48, :]
        stacked = jnp.concatenate([source, source, source], axis=0)
        return jnp.dot(features[at_block(b), :], stacked, preferred_element_type=F32)

    def values(k, b, distance):
        source = gathered[k, 32:48, :].astype(F32)
        source_area = source[13:14] + source[14:15] + source[15:16]
        reals, imags = [], []
        for q in range(128 // PIECE):
            weight = areas[at_block(b, PIECE * q, PIECE), :] * source_area
            real, imag = tile_values(distance[PIECE * q : PIECE * q + PIECE, :], weight)
            reals.append(real)
            imags.append(imag)
        return jnp.concatenate(reals, axis=0), jnp.concatenate(imags, axis=0)

    def images(k, b, real, imag):
        columns = gathered[k, 0:32, :]
        turned_columns = jnp.concatenate([-columns[16:32], columns[0:16]], axis=0)
        primal_acc[:, at_block(b)] += lax.dot_general(
            jnp.concatenate([columns, turned_columns], axis=1),
            jnp.concatenate([real, imag], axis=1),
            (((1,), (1,)), ((), ())),
            preferred_element_type=F32,
        )
        return jnp.dot(
            adjoint_pack[b], jnp.concatenate([real, imag], axis=0), preferred_element_type=F32
        )

    def process(todo, chunks):
        totals = {}
        ahead = distances(*todo[0])
        behind = None

        def finish(k, b, pair):
            term = images(k, b, *pair)
            name = chunks[id(k)]
            totals[name] = term if name not in totals else totals[name] + term

        for n, (k, b) in enumerate(todo):
            distance = ahead
            if n + 1 < len(todo):
                ahead = distances(*todo[n + 1])
            if behind is not None:
                finish(*behind)
            behind = (k, b, values(k, b, distance))
        finish(*behind)
        return totals

    def by_chunk(slots):
        chunks = {id(k): n for n, k in enumerate(slots)}
        totals = process([(k, b) for k in slots for b in range(blocks)], chunks)
        for n, k in enumerate(slots):
            adjoint_send[k] = totals[n]

    def early(slots):
        for k in slots:
            gather_copy(k).wait_recv()
        by_chunk(slots)
        for k in slots:
            adjoint_copy(k).start()

    by_chunk([0])
    pl.semaphore_wait(known_y, 2)
    greet_ring(known_z, 1)
    early([1, 2, 3])
    pl.semaphore_wait(known_z, 2)
    greet_ring(known_all, 1)
    early([4, 5, 6, 7, 8])

    rest = list(range(9, nw))
    for k in rest:
        gather_copy(k).wait_recv()
        adjoint_send[k] = jnp.zeros((32, 128), F32)
    lane = lax.broadcasted_iota(jnp.int32, (8, 128), 1) // 32

    def primal_copy(k):
        peer = lax.rem(long_at + k, nl)
        return pltpu.make_async_remote_copy(
            src_ref=primal_send.at[peer],
            dst_ref=primal_recv.at[k],
            send_sem=primal_go.at[k],
            recv_sem=primal_in.at[k],
            device_id=(wide_at, peer),
            device_id_type=MESH,
        )

    def block_step(n, carry):
        b = n + (n // 2) * (1 - 2 * (n % 2))
        totals = process([(k, b) for k in rest], {id(k): k for k in rest})
        for k in rest:
            adjoint_send[k] += totals[k]

        held = [primal_acc[8 * j : 8 * j + 8, at_block(b)] for j in range(4)]
        for q in range(4):
            piece = jnp.zeros((8, 128), F32)
            for j in range(4):
                shift = (32 * (j - q)) % 128
                moved = held[j] if shift == 0 else pltpu.roll(held[j], shift, 1)
                piece = jnp.where(lane == j, moved, piece)
            primal_send[4 * b + q] = piece

        @pl.when(b == 0)
        def _():
            pl.semaphore_wait(known_all, 2)

        for q in range(4):
            ahead = lax.rem(4 * b + q + nl - long_at, nl)

            @pl.when(ahead > 0)
            def _():
                primal_copy(ahead).start()

        return carry

    lax.fori_loop(0, blocks, block_step, 0)
    for k in rest:
        adjoint_copy(k).start()

    total = adjoint_send[0]
    for k in range(1, nw):
        adjoint_copy(k).wait_recv()
        total = total + adjoint_recv[k]
    adjoint_out[...] = total

    def finish_wide(k, carry):
        gather_copy(k).wait_send()
        adjoint_copy(k).wait_send()
        return carry

    def finish_long(k, carry):
        primal_copy(k).wait_send()
        return carry

    lax.fori_loop(1, nw, finish_wide, 0)
    lax.fori_loop(1, nl, finish_long, 0)

    total = primal_send[long_at]
    for k in range(1, nl):
        primal_copy(k).wait_recv()
        total = total + primal_recv[k]
    for j in range(4):
        primal_out[8 * j : 8 * j + 8, :] = total[:, 32 * j : 32 * j + 32]


def write_out(primal, adjoint, primal_out, adjoint_out, done):
    one = pltpu.make_async_copy(primal, primal_out, done.at[0])
    two = pltpu.make_async_copy(adjoint, adjoint_out, done.at[1])
    one.start()
    two.start()
    one.wait()
    two.wait()


def solution(mesh):
    nw, nl = mesh.shape["wide"], mesh.shape["long"]

    def shards(sv, se, xv, xe, pb, ab):
        slab_width, source_width = se.shape[1], xe.shape[1]
        far = pl.BlockSpec(memory_space=pl.ANY)
        vmem = pl.BlockSpec(memory_space=pltpu.VMEM)
        primal, adjoint = pl.pallas_call(
            functools.partial(kernel, nw, nl),
            out_shape=(
                pltpu.VMEM((32, slab_width // nl), F32),
                pltpu.VMEM((32, source_width), F32),
            ),
            in_specs=[far] * 6,
            out_specs=(vmem, vmem),
            scratch_shapes=[
                *(pltpu.VMEM(x.shape, x.dtype) for x in (sv, se, xv, xe, pb, ab)),
                pltpu.SemaphoreType.DMA((6,)),
                pltpu.VMEM((8, sv.shape[1]), F32),
                pltpu.VMEM((8, xv.shape[1]), F32),
                pltpu.VMEM((16, source_width), F32),
                pltpu.VMEM((64, slab_width), F32),
                pltpu.VMEM((slab_width, ROWS), BF16),
                pltpu.VMEM((slab_width, 128), F32),
                pltpu.VMEM((slab_width // 128, 32, 256), BF16),
                pltpu.VMEM((nw, ROWS, source_width), BF16),
                pltpu.VMEM((32, slab_width), F32),
                pltpu.VMEM((nw, 32, source_width), F32),
                pltpu.VMEM((nw, 32, source_width), F32),
                pltpu.VMEM((nl, 8, 128), F32),
                pltpu.VMEM((nl, 8, 128), F32),
                pltpu.SemaphoreType.DMA((nw,)),
                pltpu.SemaphoreType.DMA((nw,)),
                pltpu.SemaphoreType.DMA((nw,)),
                pltpu.SemaphoreType.DMA((nw,)),
                pltpu.SemaphoreType.DMA((nl,)),
                pltpu.SemaphoreType.DMA((nl,)),
                pltpu.SemaphoreType.REGULAR,
                pltpu.SemaphoreType.REGULAR,
                pltpu.SemaphoreType.REGULAR,
            ],
            compiler_params=pltpu.CompilerParams(collective_id=0, has_side_effects=True),
        )(sv, se, xv, xe, pb, ab)
        return pl.pallas_call(
            write_out,
            out_shape=(
                jax.ShapeDtypeStruct(primal.shape, F32),
                jax.ShapeDtypeStruct(adjoint.shape, F32),
            ),
            in_specs=[vmem, vmem],
            out_specs=(far, far),
            scratch_shapes=[pltpu.SemaphoreType.DMA((2,))],
        )(
            pltpu.with_memory_space_constraint(primal, pltpu.VMEM),
            pltpu.with_memory_space_constraint(adjoint, pltpu.VMEM),
        )

    return jax.shard_map(
        shards,
        mesh=mesh,
        in_specs=(
            P(None, "wide"),
            P(None, "wide"),
            P(None, ("wide", "long")),
            P(None, ("wide", "long")),
            P(None, ("wide", "long")),
            P(None, "wide"),
        ),
        out_specs=(P(None, ("wide", "long")), P(None, ("wide", "long"))),
        check_vma=False,
    )
```
